512 devices in a mesh: seq: 32 (over z, core), chan: 16 (over x, y).
Axes of the slice: x: 4, y: 4, z: 16, core: 2. Of those that a mesh axis runs over, the one named last changes fastest.
Arguments:
- loaded: bfloat16 [3, 32768, 4096], P(None, 'seq', 'chan'), may hold values from -6 to 6
- dest_tiles: int32 [1024], P('seq'), may hold values from 0 to 511, as said below
- tile_counts: int32 [32], P('seq'), may hold values from 8 to 32, as said below
- segments: int32 [16384], P('seq'), may hold values from 0 to 63, never falling along the last dimension, each value on 1 to 1024 neighbouring positions
- short_filters: float32 [3, 7, 4096], P(None, None, 'chan')
- long_filters: bfloat16 [256, 16384], P('chan', 'seq')
- skip_gain: float32 [4096], P('chan'), may hold values from 0.5 to 1.5
- norm_gain: float32 [4096], P('chan'), may hold values from 0.5 to 1.5
Outputs:
- layer_out: bfloat16 [16384, 4096], P('seq', 'chan')
The draws below stay inside these ranges and needn't reach their ends.
Inputs may be any that keep to these rules, and one draw needn't show every extreme that they name: Index s of seq holds tile_counts[s] tiles in its first slots; the busiest holds exactly 32, and every count is a multiple of 2. `dest_tiles`: entry s * 32 + j names the tile held in slot j of index s when j < tile_counts[s]; later slots name arbitrary tiles. The used slots name every tile exactly once. Tile d belongs to index d // 16 of seq, and one index holds either none or exactly 2 tiles of any one index.
All inputs are finite; a program needn't handle non-finite values.
Results may differ from the reference program's by a relative error of at most 0.0057.
Values may be sent and summed in bfloat16 or wider, within the bound.
No kernel may reach another device: no remote copies, remote signals or barrier semaphores. Data moves between devices by JAX's collectives and lax.ppermute only.
A program may use at most 64 MiB of HBM per device.

```python
import math
import jax
import jax.numpy as jnp
import numpy as np
from jax import lax

CHANNELS = 4096
GROUP_SIZE = 16
SHORT = 7
TILE = 32
TILES_DEV = 16
PACKED_TOKENS = 16384
NTILES = 512
CAP = 32
LONG_FILTER_SET = 256
DOCS = 64
N_SEQ = 32


def route_tables(key):
    devices = N_SEQ
    per_device = TILES_DEV
    pair_count = 4 * per_device // devices
    slot_count = 2 * per_device
    repeats = np.array([devices // 2, devices // 4, devices // 8, devices // 8] * (devices // 4))
    entry_total = devices * devices // 4
    entry_dst = np.arange(entry_total) % devices
    entry_rank = np.arange(entry_total) // devices
    random_subkeys = jax.random.split(jax.random.fold_in(key, 11), 5)
    src_perm = jax.random.permutation(random_subkeys[0], devices)
    dst_perm = jax.random.permutation(random_subkeys[1], devices)
    local_perm = jax.vmap(lambda sub: jax.random.permutation(sub, per_device))(jax.random.split(random_subkeys[2], devices))
    within = entry_rank[:, None] * pair_count + np.arange(pair_count)[None, :]
    tile_ids = dst_perm[entry_dst][:, None] * per_device + local_perm[entry_dst[:, None], within]
    starts = np.concatenate([[0], np.cumsum(repeats)[:-1]])
    counts_pre = repeats * pair_count
    slot_rows = []
    for source in range(devices):
        used = int(counts_pre[source])
        run_tiles = tile_ids[int(starts[source]):int(starts[source]) + int(repeats[source])].reshape(-1)
        shuffle = jax.random.permutation(jax.random.fold_in(random_subkeys[3], source), used)
        filler = jax.random.randint(jax.random.fold_in(random_subkeys[4], source), (slot_count - used,), 0, devices * per_device)
        slot_rows.append(jnp.concatenate([run_tiles[shuffle], filler]))
    slot_table = jnp.stack(slot_rows)
    inverse = jnp.argsort(src_perm)
    dest_list = slot_table[inverse].reshape(-1).astype(jnp.int32)
    count_list = jnp.asarray(counts_pre, jnp.int32)[inverse]
    return (dest_list, count_list)


def draw_dest_tiles(key, part):
    return route_tables(key)[0]


def draw_tile_counts(key, part):
    return route_tables(key)[1]


def draw_short_filters(key, part):
    random_subkeys = jax.random.split(jax.random.fold_in(key, 3), 2)
    filter_jitter = jax.random.normal(random_subkeys[0], (3, SHORT, CHANNELS))
    ramp_power = 0.5
    spread = jnp.exp(0.5 * jax.random.uniform(random_subkeys[1], (CHANNELS,), minval=0.0, maxval=math.log(10.0)))
    channel_ramp = jnp.exp(ramp_power * math.log(3.0) * jnp.arange(CHANNELS, dtype=jnp.float32) / (CHANNELS - 1))
    row_scale = jnp.stack([spread * channel_ramp, jnp.ones((CHANNELS,), jnp.float32), jnp.ones((CHANNELS,), jnp.float32)])
    return (filter_jitter * row_scale[:, None, :] / math.sqrt(SHORT)).astype(jnp.float32)


def unit_power(rate):
    return jnp.expm1(-2.0 * rate * PACKED_TOKENS) / jnp.expm1(-2.0 * rate)


def draw_long_filters(key, part):
    random_subkeys = jax.random.split(jax.random.fold_in(key, 5), 8)
    delay_index = jnp.arange(PACKED_TOKENS, dtype=jnp.float32)[None, :]
    fast_share = 0.5
    filter_jitter = jax.random.normal(random_subkeys[0], (LONG_FILTER_SET, PACKED_TOKENS))
    second_jitter = jax.random.normal(random_subkeys[5], (LONG_FILTER_SET, PACKED_TOKENS))
    fast_filter = jax.random.uniform(random_subkeys[1], (LONG_FILTER_SET, 1)) < fast_share
    fast_rate = jax.random.uniform(random_subkeys[2], (LONG_FILTER_SET, 1), minval=1.0 / 50, maxval=1.0 / 30)
    slow_rate = jax.random.uniform(random_subkeys[3], (LONG_FILTER_SET, 1), minval=0.1, maxval=1.0) / PACKED_TOKENS
    falloff_speed = jnp.where(fast_filter, fast_rate, slow_rate)
    second_rate = jax.random.uniform(random_subkeys[6], (LONG_FILTER_SET, 1), minval=0.1, maxval=1.0) / PACKED_TOKENS
    second_share = jnp.where(fast_filter, jax.random.uniform(random_subkeys[7], (LONG_FILTER_SET, 1), minval=0.05, maxval=0.15), 0.0)
    spike_position = jax.random.uniform(random_subkeys[4], (LONG_FILTER_SET, 2), minval=0.05, maxval=0.95) * PACKED_TOKENS
    spike_penalty = jnp.where(delay_index >= spike_position[:, 0:1], 0.7, 1.0) * jnp.where(delay_index >= spike_position[:, 1:2], 0.7, 1.0)
    first_part = filter_jitter * jnp.exp(-falloff_speed * delay_index) / jnp.sqrt(unit_power(falloff_speed))
    second_part = second_jitter * jnp.exp(-second_rate * delay_index) / jnp.sqrt(unit_power(second_rate))
    value_entries = (jnp.sqrt(1.0 - second_share) * first_part + jnp.sqrt(second_share) * second_part) * spike_penalty
    return value_entries.astype(jnp.bfloat16)


def block_scale(rng, shape, cuts, least, largest):
    def one(dim, shards_of):
        draws = jax.random.uniform(jax.random.fold_in(jax.random.fold_in(rng, 6), dim), (shards_of,), jnp.float32, least / len(cuts), largest / len(cuts))
        return jnp.repeat(jnp.exp(draws), shape[dim] // shards_of).reshape((-1,) + (1,) * (len(shape) - dim - 1))

    level = one(*cuts[0])
    for cut in cuts[1:]:
        level = level * one(*cut)
    return level


def split_up(number_of, total, limit, lean):
    loads = [(1 << 20) // math.isqrt(rank ** lean) + 1 for rank in range(2, number_of + 1)]
    surplus, holding = total - limit - (number_of - 1), [1] * (number_of - 1)
    while surplus > 0:
        candidates = [i for i in range(number_of - 1) if holding[i] < limit]
        whole, left = sum([loads[i] for i in candidates]), surplus
        for i in candidates:
            more = min(limit - holding[i], max(1, left * loads[i] // whole), surplus)
            holding[i] = holding[i] + more
            surplus = surplus - more
    return np.array([limit] + holding)


def uneven_parts(rng, count, total, bound, lean):
    if count == 2:
        one = jax.random.randint(rng, (), max(1, total - bound), min(bound, total - 1) + 1)
        return jnp.stack([one, total - one])
    sizes = jnp.asarray(split_up(count, total, bound, lean), jnp.int32)
    twos = (count - 1) // 2
    source_of, receiver = sizes[1:1 + 2 * twos:2], sizes[2:2 + 2 * twos:2]
    slack = jnp.minimum(source_of - 1, bound - receiver)
    shifted = jax.random.randint(jax.random.fold_in(rng, 1), (twos,), 0, 1 << 20) % (slack + 1)
    sizes = sizes.at[1:1 + 2 * twos:2].set(source_of - shifted).at[2:2 + 2 * twos:2].set(receiver + shifted)
    return sizes[jax.random.permutation(jax.random.fold_in(rng, 2), count)]


def scatter_about(stream_key, shape, scale, bound, pieces=(), kind=jnp.bfloat16):
    level = block_scale(stream_key, shape, pieces, -0.22, 0.18) if pieces else 1.0
    result = jax.random.normal(stream_key, shape, jnp.float32) * scale * level
    return jnp.minimum(jnp.maximum(result, -bound), bound).astype(kind)


def setup_inputs(seed: int = 0) -> dict:
    seeds = jax.random.split(jax.random.key(seed), 9)
    return {
        "loaded": scatter_about(seeds[0], (3, N_SEQ * CAP * TILE, CHANNELS), 1.0, 6.0, ((1, 32), (2, 16))),
        "dest_tiles": draw_dest_tiles(jax.random.fold_in(seeds[8], 71), 0),
        "tile_counts": draw_tile_counts(jax.random.fold_in(seeds[8], 71), 0),
        "segments": jnp.searchsorted(jnp.cumsum(uneven_parts(seeds[3], DOCS, PACKED_TOKENS, min(1024, PACKED_TOKENS - DOCS + 1), 2)), jnp.arange(PACKED_TOKENS), side="right").astype(jnp.int32),
        "short_filters": draw_short_filters(jax.random.fold_in(seeds[8], 71), 0),
        "long_filters": draw_long_filters(jax.random.fold_in(seeds[8], 71), 0),
        "skip_gain": jnp.clip(0.5 + 1.0 * jax.random.uniform(seeds[6], (CHANNELS,), jnp.float32) ** block_scale(seeds[6], (CHANNELS,), ((0, 16),), -0.2, 0.2), 0.5, 1.5),
        "norm_gain": jnp.clip(1.0 + 0.1 * jax.random.normal(seeds[7], (CHANNELS,), jnp.float32), 0.5, 1.5),
    }


def reference(loaded, dest_tiles, tile_counts, segments, short_filters, long_filters, skip_gain, norm_gain):
    slot_total = N_SEQ * CAP
    slot_ids = jnp.arange(slot_total, dtype=jnp.int32)
    valid_slot = slot_ids % CAP < jnp.repeat(tile_counts, CAP)
    target = jnp.where(valid_slot, dest_tiles, NTILES).astype(jnp.int32)
    holder = jnp.zeros((NTILES,), jnp.int32).at[target].set(slot_ids, mode='drop')
    same_doc = []
    for offset in range(SHORT):
        head_rows = jnp.zeros((offset,), jnp.bool_)
        same_doc.append(jnp.concatenate([head_rows, segments[offset:] == segments[:PACKED_TOKENS - offset]]))

    def one_group(group_index):
        first_column = group_index * GROUP_SIZE
        columns = lax.dynamic_slice_in_dim(loaded, first_column, GROUP_SIZE, 2)
        tile_blocks = columns.reshape(3, slot_total, TILE, GROUP_SIZE)
        arranged = jnp.take(tile_blocks, holder, axis=1).reshape(3, PACKED_TOKENS, GROUP_SIZE).astype(jnp.float32)
        tap_weights = lax.dynamic_slice_in_dim(short_filters, first_column, GROUP_SIZE, 2)
        filtered = jnp.zeros((3, PACKED_TOKENS, GROUP_SIZE), jnp.float32)
        for offset in range(SHORT):
            delayed = jnp.pad(arranged[:, :PACKED_TOKENS - offset], ((0, 0), (offset, 0), (0, 0)))
            filtered = filtered + jnp.where(same_doc[offset][None, :, None], delayed, 0.0) * tap_weights[:, offset][:, None, :]
        gate_rows = lax.optimization_barrier(filtered[0].astype(jnp.bfloat16)).astype(jnp.float32)
        mixed_rows = lax.optimization_barrier((filtered[1] * filtered[2]).astype(jnp.bfloat16)).astype(jnp.float32)
        kernel = lax.dynamic_index_in_dim(long_filters, group_index, 0, keepdims=False).astype(jnp.float32)
        spectrum = jnp.fft.rfft(mixed_rows, n=2 * PACKED_TOKENS, axis=0) * jnp.fft.rfft(kernel, n=2 * PACKED_TOKENS)[:, None]
        convolved = jnp.fft.irfft(spectrum, n=2 * PACKED_TOKENS, axis=0)[:PACKED_TOKENS]
        direct = lax.dynamic_slice_in_dim(skip_gain, first_column, GROUP_SIZE, 0)
        return gate_rows * (convolved + direct[None, :] * mixed_rows)
    gated_rows = lax.map(one_group, jnp.arange(LONG_FILTER_SET, dtype=jnp.int32))
    gated_rows = jnp.transpose(gated_rows, (1, 0, 2)).reshape(PACKED_TOKENS, CHANNELS)
    row_power = lax.optimization_barrier(jnp.mean(gated_rows * gated_rows, axis=1))
    return (gated_rows * lax.rsqrt(row_power + 1e-06)[:, None] * norm_gain[None, :]).astype(jnp.bfloat16)
```

```python
import functools

import jax
import jax.numpy as jnp
from jax import lax
from jax.experimental import pallas as pl
from jax.experimental.pallas import tpu as pltpu
from jax.sharding import PartitionSpec as P

TILE = 32
LANES = 128
TAPS = 7
f32 = jnp.float32
bf16 = jnp.bfloat16


def vmem(mib):
    return pltpu.CompilerParams(vmem_limit_bytes=mib << 20)


def turned(block):
    return jnp.transpose(block.astype(f32)).reshape(32, 8, LANES)


def pack_qk_kernel(rows_ref, extra_ref, out_ref):
    step = pl.program_id(0)

    @pl.when(step < 8)
    def _():
        both = jnp.concatenate([turned(rows_ref[0]), turned(rows_ref[1])], axis=1)
        out_ref[:, 0] = both.astype(bf16)

    @pl.when(step == 8)
    def _():
        out_ref[:, 0] = extra_ref[...]


def pack_qk(loaded, extra):
    return pl.pallas_call(
        pack_qk_kernel,
        grid=(9,),
        in_specs=[
            pl.BlockSpec((2, LANES, 256), lambda i: (0, jnp.minimum(i, 7), 0)),
            pl.BlockSpec((32, 16, LANES), lambda i: (0, 0, 0)),
        ],
        out_specs=pl.BlockSpec((32, 1, 16, LANES), lambda i: (0, i, 0, 0)),
        out_shape=jax.ShapeDtypeStruct((32, 9, 16, LANES), bf16),
        compiler_params=vmem(8),
        name="pack_qk",
    )(loaded, extra)


def pack_v_kernel(rows_ref, out_ref):
    both = jnp.concatenate(
        [turned(rows_ref[0, :LANES]), turned(rows_ref[0, LANES:])], axis=1
    )
    out_ref[:, 0] = both.astype(bf16)


def pack_v(loaded):
    return pl.pallas_call(
        pack_v_kernel,
        grid=(4,),
        in_specs=[pl.BlockSpec((1, 2 * LANES, 256), lambda i: (2, i, 0))],
        out_specs=pl.BlockSpec((32, 1, 16, LANES), lambda i: (0, i, 0, 0)),
        out_shape=jax.ShapeDtypeStruct((32, 4, 16, LANES), bf16),
        compiler_params=vmem(8),
        name="pack_v",
    )(loaded)


def gathered_column(table_ref, column, group, fetch):
    out = None
    for b in range(4):
        src = table_ref[column * 4 + b]
        tile = pltpu.roll(fetch(src), ((b - src) & 3) * TILE, 1)
        out = tile if out is None else jnp.where(group == b, tile, out)
    return out


def short_conv(block, before, reach, taps_ref, lane):
    rolled = [pltpu.roll(block, j, 1) for j in range(1, TAPS)]
    total = block * taps_ref[0]
    for j in range(1, TAPS):
        delayed = jnp.where(lane >= j, rolled[j - 1], before[j - 1])
        total = total + jnp.where(reach >= j, delayed, 0.0) * taps_ref[j]
    return total, rolled


def qk_kernel(table_ref, recv_ref, reach_ref, taps_ref, gate_ref, key_ref):
    lane = lax.broadcasted_iota(jnp.int32, (16, LANES), 1)
    group = lane // TILE

    def fetch(src):
        return recv_ref[src >> 5, (src >> 2) & 7].astype(f32)

    def step(column, before):
        block = gathered_column(table_ref, column, group, fetch)
        reach = jnp.broadcast_to(reach_ref[pl.ds(column, 1), :], (16, LANES))
        done, rolled = short_conv(block, before, reach, taps_ref, lane)
        gate_ref[column] = done[:8].astype(bf16).astype(f32)
        key_ref[column] = done[8:]
        return rolled

    zero = [jnp.zeros((16, LANES), f32)] * (TAPS - 1)
    lax.fori_loop(0, LANES, step, zero, unroll=2)


def qk_rows(table, recv, reach, taps):
    whole = pl.BlockSpec(memory_space=pltpu.VMEM)
    return pl.pallas_call(
        qk_kernel,
        in_specs=[pl.BlockSpec(memory_space=pltpu.SMEM), whole, whole, whole],
        out_specs=[whole, whole],
        out_shape=[jax.ShapeDtypeStruct((LANES, 8, LANES), f32)] * 2,
        compiler_params=vmem(8),
        name="qk_rows",
    )(table, recv, reach, taps)


def blocks_kernel(meta_ref, out_ref, lags_ref):
    lags_ref[...] = meta_ref[:, 0].astype(f32)
    row = lax.broadcasted_iota(jnp.int32, (LANES, LANES), 0)
    col = lax.broadcasted_iota(jnp.int32, (LANES, LANES), 1)
    upper = col >= row

    def step(f, before):
        for k in range(4):
            line = jnp.broadcast_to(lags_ref[f, k : k + 1, :], (LANES, LANES))
            skew = pltpu.roll(line, 0, 1, stride=1, stride_axis=0)
            block = jnp.where(upper, skew, before).astype(bf16)
            if k == 0:
                out_ref[f, 0:128, 0:128] = block
                out_ref[f, 128:256, 128:256] = block
            elif k == 1:
                out_ref[f, 0:128, 128:256] = block
                out_ref[f, 384:512, 0:128] = block
            elif k == 2:
                out_ref[f, 256:384, 0:128] = block
                out_ref[f, 384:512, 128:256] = block
            else:
                out_ref[f, 256:384, 128:256] = block

                @pl.when(f < 31)
                def _():
                    out_ref[f + 1, 128:256, 0:128] = block

            before = skew
        return before

    out_ref[0, 128:256, 0:128] = jnp.zeros((LANES, LANES), bf16)
    lax.fori_loop(0, 32, step, jnp.zeros((LANES, LANES), f32))


def toeplitz_blocks(recv):
    return pl.pallas_call(
        blocks_kernel,
        grid=(1,),
        in_specs=[pl.BlockSpec((32, 1, 16, LANES), lambda i: (0, 8, 0, 0))],
        out_specs=pl.BlockSpec((32, 512, 256), lambda i: (0, 0, 0), pipeline_mode=pl.Buffered(1)),
        out_shape=jax.ShapeDtypeStruct((32, 512, 256), bf16),
        scratch_shapes=[pltpu.VMEM((32, 16, LANES), f32)],
        compiler_params=vmem(14),
        name="toeplitz_blocks",
    )(recv)


def conv_kernel(
    table_ref, recv_ref, reach_ref, taps_ref, skip_ref, gate_ref, key_ref, blocks_ref,
    out_ref, rows_ref, acc_ref,
):
    lane = lax.broadcasted_iota(jnp.int32, (8, LANES), 1)
    group = lane // TILE
    rows_ref[0:128, :] = jnp.zeros((128, 512), bf16)

    def fetch(src):
        pair = recv_ref[src >> 5, (src >> 3) & 3].astype(f32)
        return jnp.where(((src >> 2) & 1) == 1, pair[8:], pair[:8])

    def place(u, carry):
        before, last = carry
        mixed = []
        for k in range(4):
            column = 4 * u + k
            block = gathered_column(table_ref, column, group, fetch)
            reach = jnp.broadcast_to(reach_ref[pl.ds(column, 1), :], (8, LANES))
            done, before = short_conv(block, before, reach, taps_ref, lane)
            mixed.append(done * key_ref[column])
        first = jnp.concatenate(mixed[:2], axis=1)
        second = jnp.concatenate(mixed[2:], axis=1)
        at = pl.ds(pl.multiple_of(128 + 16 * u, 16), 16)
        rows_ref[at, 0:256] = jnp.concatenate([first, second], axis=0).astype(bf16)
        rows_ref[at, 256:512] = jnp.concatenate([last, first], axis=0).astype(bf16)
        return before, second

    zero = [jnp.zeros((8, LANES), f32)] * (TAPS - 1)
    lax.fori_loop(0, 32, place, (zero, jnp.zeros((8, 256), f32)))

    for part in range(4):
        begin = 128 * part
        count = 512 - begin

        def multiply(f, carry, begin=begin, count=count, part=part):
            at = pl.multiple_of(128 + begin - 16 * f, 16)
            product = jnp.dot(
                rows_ref[pl.ds(at, count), :], blocks_ref[f], preferred_element_type=f32
            )
            if part == 0:

                @pl.when(f == 0)
                def _():
                    acc_ref[...] = product

                @pl.when(f > 0)
                def _():
                    acc_ref[...] += product

            else:
                acc_ref[begin:, :] += product
            return carry

        lax.fori_loop(8 * part, 8 * part + 8, multiply, 0)

    skip = jnp.broadcast_to(skip_ref[...], (16, 256))

    def finish(u, carry):
        at = pl.ds(pl.multiple_of(16 * u, 16), 16)
        here = pl.ds(pl.multiple_of(128 + 16 * u, 16), 16)
        total = acc_ref[at, :] + skip * rows_ref[here, 0:256].astype(f32)
        first = jnp.concatenate([gate_ref[4 * u], gate_ref[4 * u + 1]], axis=1)
        second = jnp.concatenate([gate_ref[4 * u + 2], gate_ref[4 * u + 3]], axis=1)
        out_ref[u] = (jnp.concatenate([first, second], axis=0) * total).astype(bf16)
        return carry

    lax.fori_loop(0, 32, finish, 0, unroll=2)


def conv_rows(table, recv, reach, taps, skip, gate, key, blocks):
    whole = pl.BlockSpec(memory_space=pltpu.VMEM)
    return pl.pallas_call(
        conv_kernel,
        in_specs=[pl.BlockSpec(memory_space=pltpu.SMEM)] + [whole] * 7,
        out_specs=whole,
        out_shape=jax.ShapeDtypeStruct((32, 16, 256), bf16),
        scratch_shapes=[pltpu.VMEM((640, 512), bf16), pltpu.VMEM((512, 256), f32)],
        compiler_params=vmem(20),
        name="conv_rows",
    )(table, recv, reach, taps, skip, gate, key, blocks)


def power_kernel(in_ref, out_ref):
    for half in range(2):
        block = in_ref[:, 8 * half : 8 * half + 8, :].astype(f32).reshape(256, 256)
        out_ref[half : half + 1, :] = jnp.sum(block * block, axis=0, keepdims=True)


def power_rows(rows):
    return pl.pallas_call(
        power_kernel,
        out_shape=jax.ShapeDtypeStruct((2, 256), f32),
        compiler_params=vmem(4),
        name="power_rows",
    )(rows)


def turn_kernel(in_ref, out_ref):
    for half in range(2):
        block = in_ref[:, 8 * half : 8 * half + 8, :].astype(f32).reshape(256, 256)
        out_ref[256 * half : 256 * half + 256, :] = jnp.transpose(block).astype(bf16)


def turn_rows(rows):
    return pl.pallas_call(
        turn_kernel,
        out_shape=jax.ShapeDtypeStruct((512, 256), bf16),
        compiler_params=vmem(4),
        name="turn_rows",
    )(rows)


def exchange(block, axis):
    return lax.all_to_all(block, axis, split_axis=0, concat_axis=0, tiled=True)


def local(
    loaded, dest_tiles, tile_counts, segments, short_filters, long_filters, skip_gain, norm_gain
):
    position = lax.axis_index("seq")
    lags = jnp.repeat(long_filters.reshape(16, 4, LANES), 2, axis=0)
    seg_part = jnp.broadcast_to(segments.reshape(1, 4, LANES), (32, 4, LANES)).astype(bf16)
    slots = jnp.concatenate(
        [dest_tiles // 16, dest_tiles % 16, tile_counts, jnp.zeros((63,), jnp.int32)]
    )
    slot_part = jnp.broadcast_to(slots.reshape(1, 1, LANES), (32, 1, LANES)).astype(bf16)
    extra = jnp.concatenate(
        [lags, seg_part, slot_part, jnp.zeros((32, 7, LANES), bf16)], axis=1
    )

    recv_qk = exchange(pack_qk(loaded, extra), "seq")
    recv_v = exchange(pack_v(loaded), "seq")

    known = recv_qk[:, 8].astype(f32).astype(jnp.int32)
    seg = known[:, 4:8].reshape(-1)
    placed = known[:, 8, 0:32] * 16 + known[:, 8, 32:64]
    used = jnp.arange(32, dtype=jnp.int32)[None, :] < known[:, 8, 64:65]
    placed = jnp.where(used, placed, -1).reshape(-1)
    tiles = jnp.arange(512, dtype=jnp.int32)
    slot_ids = jnp.arange(1024, dtype=jnp.int32)
    table = jnp.sum(
        jnp.where(placed[None, :] == tiles[:, None], slot_ids[None, :], 0), axis=1
    ).astype(jnp.int32)
    reach = jnp.zeros(seg.shape, jnp.int32)
    for j in range(1, TAPS):
        reach = reach + jnp.concatenate(
            [jnp.zeros((j,), jnp.int32), (seg[j:] == seg[:-j]).astype(jnp.int32)]
        )
    reach = reach.reshape(LANES, LANES)

    taps = lax.dynamic_slice_in_dim(short_filters, position * 8, 8, 2)
    taps = jnp.broadcast_to(taps[..., None], (3, TAPS, 8, LANES))
    taps_qk = jnp.transpose(taps[:2], (1, 0, 2, 3)).reshape(TAPS, 16, LANES)
    skip = lax.dynamic_slice_in_dim(skip_gain, position * 8, 8, 0)
    skip = jnp.tile(skip, 2)[:, None]

    gate, key = qk_rows(table, recv_qk, reach, taps_qk)
    blocks = toeplitz_blocks(recv_qk)
    gated = conv_rows(table, recv_v, reach, taps[2], skip, gate, key, blocks)
    mine = exchange(gated, "seq")
    power = power_rows(mine).reshape(-1)
    every = exchange(jnp.broadcast_to(power[None], (16, 512)), "chan")
    scale = lax.rsqrt(jnp.sum(every, axis=0) / 4096.0 + 1e-06)
    rows = turn_rows(mine)
    return (rows.astype(f32) * scale[:, None] * norm_gain[None, :]).astype(bf16)


def solution(mesh):
    return jax.shard_map(
        local,
        mesh=mesh,
        in_specs=(
            P(None, "seq", "chan"),
            P("seq"),
            P("seq"),
            P("seq"),
            P(None, None, "chan"),
            P("chan", "seq"),
            P("chan"),
            P("chan"),
        ),
        out_specs=P("seq", "chan"),
        check_vma=False,
    )
```

```python
import functools

import jax
import jax.numpy as jnp
from jax import lax
from jax.experimental import pallas as pl
from jax.experimental.pallas import tpu as pltpu
from jax.sharding import PartitionSpec as P

TILE = 32
LANES = 128
TAPS = 7
f32 = jnp.float32
bf16 = jnp.bfloat16


def vmem(mib):
    return pltpu.CompilerParams(vmem_limit_bytes=mib << 20)


def turned(block):
    return jnp.transpose(block.astype(f32)).reshape(32, 8, LANES)


def pack_kernel(rows_ref, out_ref):
    out_ref[:, 0] = jnp.concatenate([turned(rows_ref[t]) for t in range(3)], axis=1).astype(bf16)


def pack(loaded):
    return pl.pallas_call(
        pack_kernel,
        grid=(8,),
        in_specs=[pl.BlockSpec((3, LANES, 256), lambda i: (0, i, 0))],
        out_specs=pl.BlockSpec((32, 1, 24, LANES), lambda i: (0, i, 0, 0)),
        out_shape=jax.ShapeDtypeStruct((32, 8, 24, LANES), bf16),
        compiler_params=vmem(8),
        name="pack",
    )(loaded)


def blocks_kernel(lags_ref, out_ref):
    row = lax.broadcasted_iota(jnp.int32, (LANES, LANES), 0)
    col = lax.broadcasted_iota(jnp.int32, (LANES, LANES), 1)
    upper = col >= row

    def step(f, before):
        for k in range(8):
            line = jnp.broadcast_to(lags_ref[8 * f + k, :, :], (LANES, LANES))
            skew = pltpu.roll(line, 0, 1, stride=1, stride_axis=0)
            out_ref[8 * f + k + 1] = jnp.where(upper, skew, before).astype(bf16)
            before = skew
        return before

    out_ref[0] = jnp.zeros((LANES, LANES), bf16)
    lax.fori_loop(0, 16, step, jnp.zeros((LANES, LANES), f32))


def toeplitz_blocks(lags):
    whole = pl.BlockSpec(memory_space=pltpu.VMEM)
    return pl.pallas_call(
        blocks_kernel,
        in_specs=[whole],
        out_specs=whole,
        out_shape=jax.ShapeDtypeStruct((129, LANES, LANES), bf16),
        compiler_params=vmem(8),
        name="toeplitz_blocks",
    )(lags)


def gathered_column(table_ref, recv_ref, column, group):
    out = None
    for b in range(4):
        src = table_ref[column * 4 + b]
        tile = recv_ref[src >> 5, (src >> 2) & 7].astype(f32)
        tile = pltpu.roll(tile, ((b - src) & 3) * TILE, 1)
        out = tile if out is None else jnp.where(group == b, tile, out)
    return out


def conv_kernel(
    table_ref, recv_ref, reach_ref, taps_ref, skip_ref, lags_ref, out_ref,
    rows_ref, acc_ref, gate_ref, blocks_ref, sem,
):
    fetch = pltpu.make_async_copy(lags_ref, blocks_ref, sem)
    fetch.start()
    lane = lax.broadcasted_iota(jnp.int32, (24, LANES), 1)
    group = lane // TILE
    rows_ref[0:128, :] = jnp.zeros((128, 512), bf16)

    def place(u, carry):
        before, last = carry
        mixed = []
        gates = []
        for k in range(4):
            column = 4 * u + k
            block = gathered_column(table_ref, recv_ref, column, group)
            reach = jnp.broadcast_to(reach_ref[pl.ds(column, 1), :], (24, LANES))
            rolled = [pltpu.roll(block, j, 1) for j in range(1, TAPS)]
            total = block * taps_ref[0]
            for j in range(1, TAPS):
                delayed = jnp.where(lane >= j, rolled[j - 1], before[j - 1])
                total = total + jnp.where(reach >= j, delayed, 0.0) * taps_ref[j]
            before = rolled
            gates.append(total[:8])
            mixed.append(total[8:16] * total[16:])
        first = jnp.concatenate(mixed[:2], axis=1)
        second = jnp.concatenate(mixed[2:], axis=1)
        at = pl.ds(pl.multiple_of(128 + 16 * u, 16), 16)
        rows_ref[at, 0:256] = jnp.concatenate([first, second], axis=0).astype(bf16)
        rows_ref[at, 256:512] = jnp.concatenate([last, first], axis=0).astype(bf16)
        gate_ref[u] = jnp.concatenate(
            [jnp.concatenate(gates[:2], axis=1), jnp.concatenate(gates[2:], axis=1)], axis=0
        ).astype(bf16)
        return before, second

    zero = [jnp.zeros((24, LANES), f32)] * (TAPS - 1)
    lax.fori_loop(0, 32, place, (zero, jnp.zeros((8, 256), f32)))
    fetch.wait()

    for part in range(4):
        begin = 128 * part
        count = 512 - begin

        def multiply(f, carry, begin=begin, count=count, part=part):
            at = pl.multiple_of(128 + begin - 16 * f, 16)
            m = 4 * f
            right = jnp.concatenate(
                [
                    jnp.concatenate([blocks_ref[m + k] for k in (1, 0, 3, 2)], axis=0),
                    jnp.concatenate([blocks_ref[m + k] for k in (2, 1, 4, 3)], axis=0),
                ],
                axis=1,
            )
            product = jnp.dot(
                rows_ref[pl.ds(at, count), :], right, preferred_element_type=f32
            )
            if part == 0:

                @pl.when(f == 0)
                def _():
                    acc_ref[...] = product

                @pl.when(f > 0)
                def _():
                    acc_ref[...] += product

            else:
                acc_ref[begin:, :] += product
            return carry

        lax.fori_loop(8 * part, 8 * part + 8, multiply, 0)

    skip = jnp.broadcast_to(skip_ref[...], (16, 256))

    def finish(u, carry):
        at = pl.ds(pl.multiple_of(16 * u, 16), 16)
        here = pl.ds(pl.multiple_of(128 + 16 * u, 16), 16)
        total = acc_ref[at, :] + skip * rows_ref[here, 0:256].astype(f32)
        out_ref[u] = (gate_ref[u].astype(f32) * total).astype(bf16)
        return carry

    lax.fori_loop(0, 32, finish, 0, unroll=4)


def conv_rows(table, recv, reach, taps, skip, blocks):
    whole = pl.BlockSpec(memory_space=pltpu.VMEM)
    return pl.pallas_call(
        conv_kernel,
        in_specs=[pl.BlockSpec(memory_space=pltpu.SMEM)] + [whole] * 4
        + [pl.BlockSpec(memory_space=pltpu.HBM)],
        out_specs=whole,
        out_shape=jax.ShapeDtypeStruct((32, 16, 256), bf16),
        scratch_shapes=[
            pltpu.VMEM((640, 512), bf16),
            pltpu.VMEM((512, 256), f32),
            pltpu.VMEM((32, 16, 256), bf16),
            pltpu.VMEM((129, LANES, LANES), bf16),
            pltpu.SemaphoreType.DMA,
        ],
        compiler_params=vmem(20),
        name="conv_rows",
    )(table, recv, reach, taps, skip, blocks)


def power_kernel(in_ref, out_ref):
    for half in range(2):
        block = in_ref[:, 8 * half : 8 * half + 8, :].astype(f32).reshape(256, 256)
        out_ref[half : half + 1, :] = jnp.sum(block * block, axis=0, keepdims=True)


def power_rows(rows):
    return pl.pallas_call(
        power_kernel,
        out_shape=jax.ShapeDtypeStruct((2, 256), f32),
        compiler_params=vmem(4),
        name="power_rows",
    )(rows)


def turn_kernel(in_ref, out_ref):
    for half in range(2):
        block = in_ref[:, 8 * half : 8 * half + 8, :].astype(f32).reshape(256, 256)
        out_ref[256 * half : 256 * half + 256, :] = jnp.transpose(block).astype(bf16)


def turn_rows(rows):
    return pl.pallas_call(
        turn_kernel,
        out_shape=jax.ShapeDtypeStruct((512, 256), bf16),
        compiler_params=vmem(4),
        name="turn_rows",
    )(rows)


def exchange(block, axis):
    return lax.all_to_all(block, axis, split_axis=0, concat_axis=0, tiled=True)


def local(
    loaded, dest_tiles, tile_counts, segments, short_filters, long_filters, skip_gain, norm_gain
):
    position = lax.axis_index("seq")
    recv = exchange(pack(loaded), "seq")

    slots = jnp.concatenate(
        [dest_tiles // 16, dest_tiles % 16, tile_counts, jnp.zeros((447,), jnp.int32)]
    )
    notes = jnp.concatenate(
        [segments[None], slots[None], jnp.zeros((6, 512), jnp.int32)], axis=0
    ).astype(bf16)
    known = lax.all_gather(jnp.concatenate([long_filters, notes], axis=0), "seq")
    lags = lax.dynamic_slice_in_dim(known, position // 2, 1, 1)
    lags = lags.reshape(LANES, 1, LANES).astype(f32)
    seg = known[:, 16].astype(jnp.int32).reshape(-1)
    slots = known[:, 17].astype(jnp.int32)
    placed = slots[:, 0:32] * 16 + slots[:, 32:64]
    used = jnp.arange(32, dtype=jnp.int32)[None, :] < slots[:, 64:65]
    placed = jnp.where(used, placed, -1).reshape(-1)
    tiles = jnp.arange(512, dtype=jnp.int32)
    slot_ids = jnp.arange(1024, dtype=jnp.int32)
    table = jnp.sum(
        jnp.where(placed[None, :] == tiles[:, None], slot_ids[None, :], 0), axis=1
    ).astype(jnp.int32)
    reach = jnp.zeros(seg.shape, jnp.int32)
    for j in range(1, TAPS):
        reach = reach + jnp.concatenate(
            [jnp.zeros((j,), jnp.int32), (seg[j:] == seg[:-j]).astype(jnp.int32)]
        )
    reach = reach.reshape(LANES, LANES)

    taps = lax.dynamic_slice_in_dim(short_filters, position * 8, 8, 2)
    taps = jnp.broadcast_to(taps[..., None], (3, TAPS, 8, LANES))
    taps = jnp.transpose(taps, (1, 0, 2, 3)).reshape(TAPS, 24, LANES)
    skip = lax.dynamic_slice_in_dim(skip_gain, position * 8, 8, 0)
    skip = jnp.tile(skip, 2)[:, None]

    gated = conv_rows(table, recv, reach, taps, skip, pltpu.with_memory_space_constraint(toeplitz_blocks(lags), pltpu.HBM))
    mine = exchange(gated, "seq")
    power = power_rows(mine).reshape(-1)
    every = exchange(jnp.broadcast_to(power[None], (16, 512)), "chan")
    scale = lax.rsqrt(jnp.sum(every, axis=0) / 4096.0 + 1e-06)
    rows = turn_rows(mine)
    return (rows.astype(f32) * scale[:, None] * norm_gain[None, :]).astype(bf16)


def solution(mesh):
    return jax.shard_map(
        local,
        mesh=mesh,
        in_specs=(
            P(None, "seq", "chan"),
            P("seq"),
            P("seq"),
            P("seq"),
            P(None, None, "chan"),
            P("chan", "seq"),
            P("chan"),
            P("chan"),
        ),
        out_specs=P("seq", "chan"),
        check_vma=False,
    )
```

```python
import functools

import jax
import jax.numpy as jnp
from jax import lax
from jax.experimental import pallas as pl
from jax.experimental.pallas import tpu as pltpu
from jax.sharding import PartitionSpec as P

TILE = 32
LANES = 128
TAPS = 7
f32 = jnp.float32
bf16 = jnp.bfloat16


def vmem(mib):
    return pltpu.CompilerParams(vmem_limit_bytes=mib << 20)


def turned(block):
    return jnp.transpose(block.astype(f32)).reshape(32, 8, LANES)


def pack_kernel(
    dest_ref, count_ref, loaded_ref, lags_ref, segments_ref, out_ref,
    rows_ref, turned_ref, notes_ref, in_sems, out_sems,
):
    fetches = []
    for i in range(4):
        fetch = pltpu.make_async_copy(
            loaded_ref.at[:, pl.ds(256 * i, 256), :], rows_ref.at[i], in_sems.at[i]
        )
        fetch.start()
        fetches.append(fetch)

    lane = lax.broadcasted_iota(jnp.int32, (1, LANES), 1)
    line = jnp.zeros((1, LANES), jnp.int32)
    for j in range(32):
        high = jnp.where(j < count_ref[0], dest_ref[j] >> 4, 63)
        line = jnp.where(lane == j, high, line)
        line = jnp.where(lane == 32 + j, dest_ref[j] & 15, line)
    common = jnp.concatenate(
        [segments_ref[...].astype(f32), line.astype(f32), jnp.zeros((7, LANES), f32)], axis=0
    )
    lags = lags_ref[...].astype(f32)
    for r in range(16):
        own = [lags[r : r + 1, LANES * j : LANES * j + LANES] for j in range(4)]
        note = jnp.concatenate(own + [common], axis=0).astype(bf16)
        notes_ref[2 * r] = note
        notes_ref[2 * r + 1] = note
    sends = [
        pltpu.make_async_copy(notes_ref, out_ref.at[:, pl.ds(192, 16), :], out_sems.at[4])
    ]
    sends[0].start()

    for i in range(4):
        fetches[i].wait()
        pieces = [
            turned(rows_ref[i, t, LANES * half : LANES * half + LANES, :])
            for t in range(3)
            for half in range(2)
        ]
        turned_ref[i] = jnp.concatenate(pieces, axis=1).astype(bf16)
        send = pltpu.make_async_copy(
            turned_ref.at[i], out_ref.at[:, pl.ds(48 * i, 48), :], out_sems.at[i]
        )
        send.start()
        sends.append(send)
    for send in sends:
        send.wait()


def pack(dest, count, loaded, lags, segments):
    scalars = pl.BlockSpec(memory_space=pltpu.SMEM)
    whole = pl.BlockSpec(memory_space=pltpu.VMEM)
    far = pl.BlockSpec(memory_space=pltpu.HBM)
    return pl.pallas_call(
        pack_kernel,
        in_specs=[scalars, scalars, far, whole, whole],
        out_specs=far,
        out_shape=jax.ShapeDtypeStruct((32, 208, LANES), bf16),
        scratch_shapes=[
            pltpu.VMEM((4, 3, 256, 256), bf16),
            pltpu.VMEM((4, 32, 48, LANES), bf16),
            pltpu.VMEM((32, 16, LANES), bf16),
            pltpu.SemaphoreType.DMA((4,)),
            pltpu.SemaphoreType.DMA((5,)),
        ],
        compiler_params=vmem(12),
        name="pack",
    )(dest, count, pltpu.with_memory_space_constraint(loaded, pltpu.HBM), lags, segments)


def conv_kernel(
    table_ref, recv_ref, taps_ref, skip_ref, out_ref,
    rows_ref, acc_ref, gate_ref, blocks_ref, slots_ref, placed_ref, lags_ref, seg_ref, reach_ref,
):
    rows_ref[0:128, :] = jnp.zeros((128, 512), bf16)

    def widen(s, carry):
        for pair in range(4):
            for t in range(3):
                both = recv_ref[s, 48 * pair + 16 * t : 48 * pair + 16 * t + 16, :].astype(f32)
                slots_ref[8 * s + 2 * pair, 8 * t : 8 * t + 8, :] = both[:8]
                slots_ref[8 * s + 2 * pair + 1, 8 * t : 8 * t + 8, :] = both[8:]
        return carry

    lax.fori_loop(0, 32, widen, 0, unroll=2)
    for s in range(32):
        both = recv_ref[s, 192:208, :].astype(f32)
        lags_ref[s] = both[:8]
        seg_ref[4 * s : 4 * s + 4, :] = both[4:8]

    row = lax.broadcasted_iota(jnp.int32, (LANES, LANES), 0)
    col = lax.broadcasted_iota(jnp.int32, (LANES, LANES), 1)
    seg = seg_ref[...]
    above = pltpu.roll(seg, 1, 0)
    reach = jnp.zeros((LANES, LANES), f32)
    for j in range(1, TAPS):
        delayed = jnp.where(col >= j, pltpu.roll(seg, j, 1), pltpu.roll(above, j, 1))
        inside = (row > 0) | (col >= j)
        reach = reach + jnp.where((delayed == seg) & inside, 1.0, 0.0)
    reach_ref[...] = reach

    upper = col >= row

    def skewed(f, before):
        for k in range(8):
            line = jnp.broadcast_to(lags_ref[2 * f + k // 4, k % 4 : k % 4 + 1, :], (LANES, LANES))
            skew = pltpu.roll(line, 0, 1, stride=1, stride_axis=0)
            blocks_ref[8 * f + k + 1] = jnp.where(upper, skew, before).astype(bf16)
            before = skew
        return before

    blocks_ref[0] = jnp.zeros((LANES, LANES), bf16)
    lax.fori_loop(0, 16, skewed, jnp.zeros((LANES, LANES), f32))

    lane = lax.broadcasted_iota(jnp.int32, (24, LANES), 1)
    group = lane // TILE

    def gather(u, carry):
        for k in range(16):
            column = 16 * u + k
            out = None
            for b in range(4):
                src = table_ref[column * 4 + b]
                tile = pltpu.roll(slots_ref[src >> 2], ((b - src) & 3) * TILE, 1)
                out = tile if out is None else jnp.where(group == b, tile, out)
            placed_ref[column] = out
        return carry

    lax.fori_loop(0, 8, gather, 0)

    def short(u, carry):
        before, last = carry
        mixed = []
        gates = []
        for k in range(4):
            column = 4 * u + k
            block = placed_ref[column]
            limit = jnp.broadcast_to(reach_ref[pl.ds(column, 1), :], (24, LANES))
            rolled = [pltpu.roll(block, j, 1) for j in range(1, TAPS)]
            total = block * taps_ref[0]
            for j in range(1, TAPS):
                delayed = jnp.where(lane >= j, rolled[j - 1], before[j - 1])
                total = total + jnp.where(limit >= j, delayed, 0.0) * taps_ref[j]
            before = rolled
            gates.append(total[:8])
            mixed.append(total[8:16] * total[16:])
        first = jnp.concatenate(mixed[:2], axis=1)
        second = jnp.concatenate(mixed[2:], axis=1)
        at = pl.ds(pl.multiple_of(128 + 16 * u, 16), 16)
        rows_ref[at, 0:256] = jnp.concatenate([first, second], axis=0).astype(bf16)
        rows_ref[at, 256:512] = jnp.concatenate([last, first], axis=0).astype(bf16)
        gate_ref[u] = jnp.concatenate(
            [jnp.concatenate(gates[:2], axis=1), jnp.concatenate(gates[2:], axis=1)], axis=0
        ).astype(bf16)
        return before, second

    zero = [jnp.zeros((24, LANES), f32)] * (TAPS - 1)
    lax.fori_loop(0, 32, short, (zero, jnp.zeros((8, 256), f32)), unroll=2)

    for part in range(4):
        begin = 128 * part
        for f in range(8 * part, 8 * part + 8, 2):
            left, right = [], []
            for g in (f, f + 1):
                at = 128 + begin - 16 * g
                left.append(rows_ref[at : at + 512 - begin, :])
                right.append(
                    jnp.concatenate(
                        [
                            jnp.concatenate([blocks_ref[4 * g + k] for k in (1, 0, 3, 2)], axis=0),
                            jnp.concatenate([blocks_ref[4 * g + k] for k in (2, 1, 4, 3)], axis=0),
                        ],
                        axis=1,
                    )
                )
            product = jnp.dot(
                jnp.concatenate(left, axis=1),
                jnp.concatenate(right, axis=0),
                preferred_element_type=f32,
            )
            if f == 0:
                acc_ref[...] = product
            else:
                acc_ref[begin:, :] += product

    skip = jnp.broadcast_to(skip_ref[...], (16, 256))

    def finish(u, carry):
        at = pl.ds(pl.multiple_of(16 * u, 16), 16)
        here = pl.ds(pl.multiple_of(128 + 16 * u, 16), 16)
        total = acc_ref[at, :] + skip * rows_ref[here, 0:256].astype(f32)
        out_ref[u] = (gate_ref[u].astype(f32) * total).astype(bf16)
        return carry

    lax.fori_loop(0, 32, finish, 0, unroll=4)


def conv_rows(table, recv, taps, skip):
    whole = pl.BlockSpec(memory_space=pltpu.VMEM)
    return pl.pallas_call(
        conv_kernel,
        in_specs=[pl.BlockSpec(memory_space=pltpu.SMEM)] + [whole] * 3,
        out_specs=whole,
        out_shape=jax.ShapeDtypeStruct((32, 16, 256), bf16),
        scratch_shapes=[
            pltpu.VMEM((640, 512), bf16),
            pltpu.VMEM((512, 256), f32),
            pltpu.VMEM((32, 16, 256), bf16),
            pltpu.VMEM((129, LANES, LANES), bf16),
            pltpu.VMEM((256, 24, LANES), f32),
            pltpu.VMEM((LANES, 24, LANES), f32),
            pltpu.VMEM((32, 8, LANES), f32),
            pltpu.VMEM((LANES, LANES), f32),
            pltpu.VMEM((LANES, LANES), f32),
        ],
        compiler_params=vmem(24),
        name="conv_rows",
    )(table, recv, taps, skip)


def power_kernel(in_ref, out_ref):
    for half in range(2):
        block = in_ref[:, 8 * half : 8 * half + 8, :].astype(f32).reshape(256, 256)
        out_ref[half : half + 1, :] = jnp.sum(block * block, axis=0, keepdims=True)


def power_rows(rows):
    return pl.pallas_call(
        power_kernel,
        out_shape=jax.ShapeDtypeStruct((2, 256), f32),
        compiler_params=vmem(4),
        name="power_rows",
    )(rows)


def turn_kernel(in_ref, out_ref):
    for half in range(2):
        block = in_ref[:, 8 * half : 8 * half + 8, :].astype(f32).reshape(256, 256)
        out_ref[256 * half : 256 * half + 256, :] = jnp.transpose(block).astype(bf16)


def turn_rows(rows):
    return pl.pallas_call(
        turn_kernel,
        out_shape=jax.ShapeDtypeStruct((512, 256), bf16),
        compiler_params=vmem(4),
        name="turn_rows",
    )(rows)


def exchange(block, axis):
    return lax.all_to_all(block, axis, split_axis=0, concat_axis=0, tiled=True)


def local(
    loaded, dest_tiles, tile_counts, segments, short_filters, long_filters, skip_gain, norm_gain
):
    position = lax.axis_index("seq")
    recv = exchange(
        pack(dest_tiles, tile_counts, loaded, long_filters, segments.reshape(4, LANES)), "seq"
    )

    slots = recv[:, 200].astype(jnp.int32)
    placed = (slots[:, 0:32] * 16 + slots[:, 32:64]).reshape(-1)
    tiles = jnp.arange(512, dtype=jnp.int32)
    slot_ids = jnp.arange(1024, dtype=jnp.int32)
    table = jnp.sum(
        jnp.where(placed[None, :] == tiles[:, None], slot_ids[None, :], 0), axis=1
    ).astype(jnp.int32)

    taps = lax.dynamic_slice_in_dim(short_filters, position * 8, 8, 2)
    taps = jnp.broadcast_to(taps[..., None], (3, TAPS, 8, LANES))
    taps = jnp.transpose(taps, (1, 0, 2, 3)).reshape(TAPS, 24, LANES)
    skip = lax.dynamic_slice_in_dim(skip_gain, position * 8, 8, 0)
    skip = jnp.tile(skip, 2)[:, None]

    gated = conv_rows(table, recv, taps, skip)
    mine = exchange(gated, "seq")
    power = power_rows(mine).reshape(-1)
    every = exchange(jnp.broadcast_to(power[None], (16, 512)), "chan")
    scale = lax.rsqrt(jnp.sum(every, axis=0) / 4096.0 + 1e-06)
    rows = turn_rows(mine)
    return (rows.astype(f32) * scale[:, None] * norm_gain[None, :]).astype(bf16)


def solution(mesh):
    return jax.shard_map(
        local,
        mesh=mesh,
        in_specs=(
            P(None, "seq", "chan"),
            P("seq"),
            P("seq"),
            P("seq"),
            P(None, None, "chan"),
            P("chan", "seq"),
            P("chan"),
            P("chan"),
        ),
        out_specs=P("seq", "chan"),
        check_vma=False,
    )
```

```python
import functools

import jax
import jax.numpy as jnp
from jax import lax
from jax.experimental import pallas as pl
from jax.experimental.pallas import tpu as pltpu
from jax.sharding import PartitionSpec as P

TILE = 32
LANES = 128
TAPS = 7
f32 = jnp.float32
bf16 = jnp.bfloat16


def vmem(mib):
    return pltpu.CompilerParams(vmem_limit_bytes=mib << 20)


def turned(block):
    return jnp.transpose(block.astype(f32)).reshape(32, 8, LANES)


def pack_kernel(
    dest_hbm, count_ref, loaded_ref, lags_hbm, segments_hbm, out_ref,
    rows_ref, turned_ref, notes_ref, dest_ref, lags_ref, segments_ref,
    in_sems, out_sems, note_sems,
):
    fetches = []
    small = [
        pltpu.make_async_copy(dest_hbm, dest_ref, note_sems.at[0]),
        pltpu.make_async_copy(lags_hbm, lags_ref, note_sems.at[1]),
        pltpu.make_async_copy(segments_hbm, segments_ref, note_sems.at[2]),
    ]
    for copy in small:
        copy.start()
    for i in range(4):
        fetch = pltpu.make_async_copy(
            loaded_ref.at[:, pl.ds(256 * i, 256), :], rows_ref.at[i], in_sems.at[i]
        )
        fetch.start()
        fetches.append(fetch)

    for copy in small:
        copy.wait()
    lane = lax.broadcasted_iota(jnp.int32, (1, LANES), 1)
    line = jnp.zeros((1, LANES), jnp.int32)
    for j in range(32):
        high = jnp.where(j < count_ref[0], dest_ref[j] >> 4, 63)
        line = jnp.where(lane == j, high, line)
        line = jnp.where(lane == 32 + j, dest_ref[j] & 15, line)
    common = jnp.concatenate(
        [segments_ref[...].astype(f32), line.astype(f32), jnp.zeros((7, LANES), f32)], axis=0
    )
    lags = lags_ref[...].astype(f32)
    for r in range(16):
        own = [lags[r : r + 1, LANES * j : LANES * j + LANES] for j in range(4)]
        note = jnp.concatenate(own + [common], axis=0).astype(bf16)
        notes_ref[2 * r] = note
        notes_ref[2 * r + 1] = note
    sends = [
        pltpu.make_async_copy(notes_ref, out_ref.at[:, pl.ds(192, 16), :], out_sems.at[4])
    ]
    sends[0].start()

    for i in range(4):
        fetches[i].wait()
        pieces = [
            turned(rows_ref[i, t, LANES * half : LANES * half + LANES, :])
            for t in range(3)
            for half in range(2)
        ]
        turned_ref[i] = jnp.concatenate(pieces, axis=1).astype(bf16)
        send = pltpu.make_async_copy(
            turned_ref.at[i], out_ref.at[:, pl.ds(48 * i, 48), :], out_sems.at[i]
        )
        send.start()
        sends.append(send)
    for send in sends:
        send.wait()


def pack(dest, count, loaded, lags, segments):
    scalars = pl.BlockSpec(memory_space=pltpu.SMEM)
    far = pl.BlockSpec(memory_space=pltpu.HBM)
    dest, loaded, lags, segments = [
        pltpu.with_memory_space_constraint(a, pltpu.HBM) for a in (dest, loaded, lags, segments)
    ]
    return pl.pallas_call(
        pack_kernel,
        in_specs=[far, scalars, far, far, far],
        out_specs=far,
        out_shape=jax.ShapeDtypeStruct((32, 208, LANES), bf16),
        scratch_shapes=[
            pltpu.VMEM((4, 3, 256, 256), bf16),
            pltpu.VMEM((4, 32, 48, LANES), bf16),
            pltpu.VMEM((32, 16, LANES), bf16),
            pltpu.SMEM((32,), jnp.int32),
            pltpu.VMEM((16, 512), bf16),
            pltpu.VMEM((4, LANES), jnp.int32),
            pltpu.SemaphoreType.DMA((4,)),
            pltpu.SemaphoreType.DMA((5,)),
            pltpu.SemaphoreType.DMA((3,)),
        ],
        compiler_params=vmem(12),
        name="pack",
    )(dest, count, loaded, lags, segments)


def conv_kernel(
    table_ref, recv_ref, taps_ref, skip_ref, out_ref,
    rows_ref, acc_ref, gate_ref, blocks_ref, slots_ref, placed_ref, lags_ref, seg_ref, reach_ref,
):
    rows_ref[0:128, :] = jnp.zeros((128, 512), bf16)

    def widen(s, carry):
        for pair in range(4):
            for t in range(3):
                both = recv_ref[s, 48 * pair + 16 * t : 48 * pair + 16 * t + 16, :].astype(f32)
                slots_ref[8 * s + 2 * pair, 8 * t : 8 * t + 8, :] = both[:8]
                slots_ref[8 * s + 2 * pair + 1, 8 * t : 8 * t + 8, :] = both[8:]
        return carry

    lax.fori_loop(0, 32, widen, 0, unroll=2)
    for s in range(32):
        both = recv_ref[s, 192:208, :].astype(f32)
        lags_ref[s] = both[:8]
        seg_ref[4 * s : 4 * s + 4, :] = both[4:8]

    row = lax.broadcasted_iota(jnp.int32, (LANES, LANES), 0)
    col = lax.broadcasted_iota(jnp.int32, (LANES, LANES), 1)
    seg = seg_ref[...]
    above = pltpu.roll(seg, 1, 0)
    reach = jnp.zeros((LANES, LANES), f32)
    for j in range(1, TAPS):
        delayed = jnp.where(col >= j, pltpu.roll(seg, j, 1), pltpu.roll(above, j, 1))
        inside = (row > 0) | (col >= j)
        reach = reach + jnp.where((delayed == seg) & inside, 1.0, 0.0)
    reach_ref[...] = reach

    lane = lax.broadcasted_iota(jnp.int32, (24, LANES), 1)
    group = lane // TILE

    def gather(u, carry):
        for k in range(16):
            column = 16 * u + k
            out = None
            for b in range(4):
                src = table_ref[column * 4 + b]
                tile = pltpu.roll(slots_ref[src >> 2], ((b - src) & 3) * TILE, 1)
                out = tile if out is None else jnp.where(group == b, tile, out)
            placed_ref[column] = out
        return carry

    lax.fori_loop(0, 8, gather, 0)

    def short(u, carry):
        before, last = carry
        mixed = []
        gates = []
        for k in range(4):
            column = 4 * u + k
            block = placed_ref[column]
            limit = jnp.broadcast_to(reach_ref[pl.ds(column, 1), :], (24, LANES))
            rolled = [pltpu.roll(block, j, 1) for j in range(1, TAPS)]
            total = block * taps_ref[0]
            for j in range(1, TAPS):
                delayed = jnp.where(lane >= j, rolled[j - 1], before[j - 1])
                total = total + jnp.where(limit >= j, delayed, 0.0) * taps_ref[j]
            before = rolled
            gates.append(total[:8])
            mixed.append(total[8:16] * total[16:])
        first = jnp.concatenate(mixed[:2], axis=1)
        second = jnp.concatenate(mixed[2:], axis=1)
        at = pl.ds(pl.multiple_of(128 + 16 * u, 16), 16)
        rows_ref[at, 0:256] = jnp.concatenate([first, second], axis=0).astype(bf16)
        rows_ref[at, 256:512] = jnp.concatenate([last, first], axis=0).astype(bf16)
        gate_ref[u] = jnp.concatenate(
            [jnp.concatenate(gates[:2], axis=1), jnp.concatenate(gates[2:], axis=1)], axis=0
        ).astype(bf16)
        return before, second

    zero = [jnp.zeros((24, LANES), f32)] * (TAPS - 1)
    lax.fori_loop(0, 32, short, (zero, jnp.zeros((8, 256), f32)), unroll=4)


    upper = col >= row
    skew = jnp.zeros((LANES, LANES), f32)
    block = jnp.zeros((LANES, LANES), bf16)
    for part in range(4):
        begin = 128 * part
        for f in range(8 * part, 8 * part + 8, 2):
            left, right = [], []
            for g in (f, f + 1):
                at = 128 + begin - 16 * g
                left.append(rows_ref[at : at + 512 - begin, :])
                made = [block]
                for k in range(4):
                    line = jnp.broadcast_to(lags_ref[g, k : k + 1, :], (LANES, LANES))
                    before, skew = skew, pltpu.roll(line, 0, 1, stride=1, stride_axis=0)
                    made.append(jnp.where(upper, skew, before).astype(bf16))
                block = made[4]
                right.append(
                    jnp.concatenate(
                        [
                            jnp.concatenate([made[k] for k in (1, 0, 3, 2)], axis=0),
                            jnp.concatenate([made[k] for k in (2, 1, 4, 3)], axis=0),
                        ],
                        axis=1,
                    )
                )
            product = jnp.dot(
                jnp.concatenate(left, axis=1),
                jnp.concatenate(right, axis=0),
                preferred_element_type=f32,
            )
            if f == 0:
                acc_ref[...] = product
            else:
                acc_ref[begin:, :] += product

    skip = jnp.broadcast_to(skip_ref[...], (16, 256))

    def finish(u, carry):
        at = pl.ds(pl.multiple_of(16 * u, 16), 16)
        here = pl.ds(pl.multiple_of(128 + 16 * u, 16), 16)
        total = acc_ref[at, :] + skip * rows_ref[here, 0:256].astype(f32)
        out_ref[u] = (gate_ref[u].astype(f32) * total).astype(bf16)
        return carry

    lax.fori_loop(0, 32, finish, 0, unroll=4)


def conv_rows(table, recv, taps, skip):
    whole = pl.BlockSpec(memory_space=pltpu.VMEM)
    return pl.pallas_call(
        conv_kernel,
        in_specs=[pl.BlockSpec(memory_space=pltpu.SMEM)] + [whole] * 3,
        out_specs=whole,
        out_shape=jax.ShapeDtypeStruct((32, 16, 256), bf16),
        scratch_shapes=[
            pltpu.VMEM((640, 512), bf16),
            pltpu.VMEM((512, 256), f32),
            pltpu.VMEM((32, 16, 256), bf16),
            pltpu.VMEM((129, LANES, LANES), bf16),
            pltpu.VMEM((256, 24, LANES), f32),
            pltpu.VMEM((LANES, 24, LANES), f32),
            pltpu.VMEM((32, 8, LANES), f32),
            pltpu.VMEM((LANES, LANES), f32),
            pltpu.VMEM((LANES, LANES), f32),
        ],
        compiler_params=vmem(24),
        name="conv_rows",
    )(table, recv, taps, skip)


def power_kernel(in_ref, out_ref):
    halves = []
    for half in range(2):
        block = in_ref[:, 8 * half : 8 * half + 8, :].astype(f32).reshape(256, 256)
        halves.append(jnp.sum(block * block, axis=0, keepdims=True))
    line = jnp.concatenate(halves, axis=1)
    for i in range(16):
        out_ref[i] = line


def power_rows(rows):
    return pl.pallas_call(
        power_kernel,
        out_shape=jax.ShapeDtypeStruct((16, 1, 512), f32),
        compiler_params=vmem(4),
        name="power_rows",
    )(rows)


def scale_kernel(in_ref, power_ref, gain_ref, out_ref):
    power = jnp.sum(power_ref[...], axis=0)
    scale = lax.rsqrt(power / 4096.0 + 1e-06)
    gain = gain_ref[...]
    for half in range(2):
        block = in_ref[:, 8 * half : 8 * half + 8, :].astype(f32).reshape(256, 256)
        block = block * scale[:, 256 * half : 256 * half + 256] * gain
        out_ref[256 * half : 256 * half + 256, :] = jnp.transpose(block).astype(bf16)


def scale_rows(rows, power, gain):
    return pl.pallas_call(
        scale_kernel,
        out_shape=jax.ShapeDtypeStruct((512, 256), bf16),
        compiler_params=vmem(4),
        name="scale_rows",
    )(rows, power, gain)


def exchange(block, axis):
    return lax.all_to_all(block, axis, split_axis=0, concat_axis=0, tiled=True)


def local(
    loaded, dest_tiles, tile_counts, segments, short_filters, long_filters, skip_gain, norm_gain
):
    position = lax.axis_index("seq")
    recv = exchange(
        pack(dest_tiles, tile_counts, loaded, long_filters, segments.reshape(4, LANES)), "seq"
    )

    slots = recv[:, 200].astype(jnp.int32)
    placed = (slots[:, 0:32] * 16 + slots[:, 32:64]).reshape(-1)
    tiles = jnp.arange(512, dtype=jnp.int32)
    slot_ids = jnp.arange(1024, dtype=jnp.int32)
    table = jnp.sum(
        jnp.where(placed[None, :] == tiles[:, None], slot_ids[None, :], 0), axis=1
    ).astype(jnp.int32)

    taps = lax.dynamic_slice_in_dim(short_filters, position * 8, 8, 2)
    taps = jnp.broadcast_to(taps[..., None], (3, TAPS, 8, LANES))
    taps = jnp.transpose(taps, (1, 0, 2, 3)).reshape(TAPS, 24, LANES)
    skip = lax.dynamic_slice_in_dim(skip_gain, position * 8, 8, 0)
    skip = jnp.tile(skip, 2)[:, None]

    gated = conv_rows(table, recv, taps, skip)
    mine = exchange(gated, "seq")
    every = exchange(power_rows(mine), "chan")
    return scale_rows(mine, every, norm_gain[:, None])


def solution(mesh):
    return jax.shard_map(
        local,
        mesh=mesh,
        in_specs=(
            P(None, "seq", "chan"),
            P("seq"),
            P("seq"),
            P("seq"),
            P(None, None, "chan"),
            P("chan", "seq"),
            P("chan"),
            P("chan"),
        ),
        out_specs=P("seq", "chan"),
        check_vma=False,
    )
```

```python
import functools

import jax
import jax.numpy as jnp
from jax import lax
from jax.experimental import pallas as pl
from jax.experimental.pallas import tpu as pltpu
from jax.sharding import PartitionSpec as P

TILE = 32
LANES = 128
TAPS = 7
f32 = jnp.float32
bf16 = jnp.bfloat16


def vmem(mib):
    return pltpu.CompilerParams(vmem_limit_bytes=mib << 20)


def turned(block):
    return jnp.transpose(block.astype(f32)).reshape(32, 8, LANES)


def pack_kernel(
    dest_hbm, count_ref, loaded_ref, lags_hbm, segments_hbm, out_ref,
    rows_ref, turned_ref, notes_ref, dest_ref, lags_ref, segments_ref,
    in_sems, out_sems, note_sems,
):
    fetches = []
    small = [
        pltpu.make_async_copy(dest_hbm, dest_ref, note_sems.at[0]),
        pltpu.make_async_copy(lags_hbm, lags_ref, note_sems.at[1]),
        pltpu.make_async_copy(segments_hbm, segments_ref, note_sems.at[2]),
    ]
    for copy in small:
        copy.start()
    for i in range(4):
        fetch = pltpu.make_async_copy(
            loaded_ref.at[:, pl.ds(256 * i, 256), :], rows_ref.at[i], in_sems.at[i]
        )
        fetch.start()
        fetches.append(fetch)

    for copy in small:
        copy.wait()
    lane = lax.broadcasted_iota(jnp.int32, (1, LANES), 1)
    line = jnp.zeros((1, LANES), jnp.int32)
    for j in range(32):
        high = jnp.where(j < count_ref[0], dest_ref[j] >> 4, 63)
        line = jnp.where(lane == j, high, line)
        line = jnp.where(lane == 32 + j, dest_ref[j] & 15, line)
    index = lax.broadcasted_iota(jnp.int32, (LANES, LANES), 0)
    fewer = jnp.zeros((LANES, LANES), f32)
    for j in range(4):
        fewer = fewer + jnp.where(segments_ref[j : j + 1, :] < (index & 63), 1.0, 0.0)
    below = jnp.sum(fewer, axis=1, keepdims=True).astype(jnp.int32)
    below = jnp.where(index[:, :1] < 64, below >> 4, below & 15).astype(f32)
    below = jnp.transpose(jnp.broadcast_to(below, (LANES, LANES)))[:1]
    common = jnp.concatenate([below, line.astype(f32), jnp.zeros((2, LANES), f32)], axis=0)
    lags = lags_ref[...].astype(f32)
    for r in range(16):
        own = [lags[r : r + 1, LANES * j : LANES * j + LANES] for j in range(4)]
        note = jnp.concatenate(own + [common], axis=0).astype(bf16)
        notes_ref[2 * r] = note
        notes_ref[2 * r + 1] = note
    sends = [
        pltpu.make_async_copy(notes_ref, out_ref.at[:, pl.ds(192, 8), :], out_sems.at[4])
    ]
    sends[0].start()

    for i in range(4):
        fetches[i].wait()
        pieces = [
            turned(rows_ref[i, t, LANES * half : LANES * half + LANES, :])
            for t in range(3)
            for half in range(2)
        ]
        turned_ref[i] = jnp.concatenate(pieces, axis=1).astype(bf16)
        send = pltpu.make_async_copy(
            turned_ref.at[i], out_ref.at[:, pl.ds(48 * i, 48), :], out_sems.at[i]
        )
        send.start()
        sends.append(send)
    for send in sends:
        send.wait()


def pack(dest, count, loaded, lags, segments):
    scalars = pl.BlockSpec(memory_space=pltpu.SMEM)
    far = pl.BlockSpec(memory_space=pltpu.HBM)
    dest, loaded, lags, segments = [
        pltpu.with_memory_space_constraint(a, pltpu.HBM) for a in (dest, loaded, lags, segments)
    ]
    return pl.pallas_call(
        pack_kernel,
        in_specs=[far, scalars, far, far, far],
        out_specs=far,
        out_shape=jax.ShapeDtypeStruct((32, 200, LANES), bf16),
        scratch_shapes=[
            pltpu.VMEM((4, 3, 256, 256), bf16),
            pltpu.VMEM((4, 32, 48, LANES), bf16),
            pltpu.VMEM((32, 8, LANES), bf16),
            pltpu.SMEM((32,), jnp.int32),
            pltpu.VMEM((16, 512), bf16),
            pltpu.VMEM((4, LANES), jnp.int32),
            pltpu.SemaphoreType.DMA((4,)),
            pltpu.SemaphoreType.DMA((5,)),
            pltpu.SemaphoreType.DMA((3,)),
        ],
        compiler_params=vmem(12),
        name="pack",
    )(dest, count, loaded, lags, segments)


def conv_kernel(
    table_ref, recv_ref, taps_ref, skip_ref, out_ref,
    rows_ref, acc_ref, gate_ref, slots_ref, placed_ref, lags_ref, starts_ref, reach_ref,
):
    rows_ref[0:128, :] = jnp.zeros((128, 512), bf16)

    def widen(s, carry):
        for pair in range(4):
            for t in range(3):
                both = recv_ref[s, 48 * pair + 16 * t : 48 * pair + 16 * t + 16, :].astype(f32)
                slots_ref[8 * s + 2 * pair, 8 * t : 8 * t + 8, :] = both[:8]
                slots_ref[8 * s + 2 * pair + 1, 8 * t : 8 * t + 8, :] = both[8:]
        return carry

    lax.fori_loop(0, 32, widen, 0, unroll=2)
    total = jnp.zeros((8, LANES), f32)
    for s in range(32):
        note = recv_ref[s, 192:200, :].astype(f32)
        lags_ref[s] = note
        total = total + note

    starts = 16.0 * total[4:5] + pltpu.roll(total[4:5], 64, 1)
    starts_ref[...] = jnp.transpose(jnp.broadcast_to(starts, (LANES, LANES)))
    row = lax.broadcasted_iota(jnp.int32, (LANES, LANES), 0)
    col = lax.broadcasted_iota(jnp.int32, (LANES, LANES), 1)
    here = (row * LANES + col).astype(f32)

    def latest(v, begin):
        for k in range(8):
            start = jnp.broadcast_to(starts_ref[pl.ds(8 * v + k, 1), :], (LANES, LANES))
            begin = jnp.where(start <= here, start, begin)
        return begin

    begin = lax.fori_loop(0, 8, latest, jnp.zeros((LANES, LANES), f32))
    reach_ref[...] = jnp.minimum(here - begin, 6.0)

    lane = lax.broadcasted_iota(jnp.int32, (24, LANES), 1)
    group = lane // TILE

    def gather(u, carry):
        for k in range(32):
            column = 32 * u + k
            out = None
            for b in range(4):
                src = table_ref[column * 4 + b]
                tile = pltpu.roll(slots_ref[src >> 2], ((b - src) & 3) * TILE, 1)
                out = tile if out is None else jnp.where(group == b, tile, out)
            placed_ref[column] = out
        return carry

    lax.fori_loop(0, 4, gather, 0)

    def short(u, carry):
        before, last = carry
        mixed = []
        gates = []
        for k in range(4):
            column = 4 * u + k
            block = placed_ref[column]
            limit = jnp.broadcast_to(reach_ref[pl.ds(column, 1), :], (24, LANES))
            rolled = [pltpu.roll(block, j, 1) for j in range(1, TAPS)]
            total = block * taps_ref[0]
            for j in range(1, TAPS):
                delayed = jnp.where(lane >= j, rolled[j - 1], before[j - 1])
                total = total + jnp.where(limit >= j, delayed, 0.0) * taps_ref[j]
            before = rolled
            gates.append(total[:8])
            mixed.append(total[8:16] * total[16:])
        first = jnp.concatenate(mixed[:2], axis=1)
        second = jnp.concatenate(mixed[2:], axis=1)
        at = pl.ds(pl.multiple_of(128 + 16 * u, 16), 16)
        rows_ref[at, 0:256] = jnp.concatenate([first, second], axis=0).astype(bf16)
        rows_ref[at, 256:512] = jnp.concatenate([last, first], axis=0).astype(bf16)
        gate_ref[u] = jnp.concatenate(
            [jnp.concatenate(gates[:2], axis=1), jnp.concatenate(gates[2:], axis=1)], axis=0
        ).astype(bf16)
        return before, second

    zero = [jnp.zeros((24, LANES), f32)] * (TAPS - 1)
    lax.fori_loop(0, 32, short, (zero, jnp.zeros((8, 256), f32)), unroll=16)


    upper = col >= row
    skew = jnp.zeros((LANES, LANES), f32)
    block = jnp.zeros((LANES, LANES), bf16)
    for part in range(4):
        begin = 128 * part
        for f in range(8 * part, 8 * part + 8, 2):
            left, right = [], []
            for g in (f, f + 1):
                at = 128 + begin - 16 * g
                left.append(rows_ref[at : at + 512 - begin, :])
                made = [block]
                for k in range(4):
                    line = jnp.broadcast_to(lags_ref[g, k : k + 1, :], (LANES, LANES))
                    before, skew = skew, pltpu.roll(line, 0, 1, stride=1, stride_axis=0)
                    made.append(jnp.where(upper, skew, before).astype(bf16))
                block = made[4]
                right.append(
                    jnp.concatenate(
                        [
                            jnp.concatenate([made[k] for k in (1, 0, 3, 2)], axis=0),
                            jnp.concatenate([made[k] for k in (2, 1, 4, 3)], axis=0),
                        ],
                        axis=1,
                    )
                )
            product = jnp.dot(
                jnp.concatenate(left, axis=1),
                jnp.concatenate(right, axis=0),
                preferred_element_type=f32,
            )
            if f == 0:
                acc_ref[...] = product
            else:
                acc_ref[begin:, :] += product

    skip = jnp.broadcast_to(skip_ref[...], (16, 256))

    def finish(u, carry):
        at = pl.ds(pl.multiple_of(16 * u, 16), 16)
        here = pl.ds(pl.multiple_of(128 + 16 * u, 16), 16)
        total = acc_ref[at, :] + skip * rows_ref[here, 0:256].astype(f32)
        out_ref[u] = (gate_ref[u].astype(f32) * total).astype(bf16)
        return carry

    lax.fori_loop(0, 32, finish, 0, unroll=4)


def conv_rows(table, recv, taps, skip):
    whole = pl.BlockSpec(memory_space=pltpu.VMEM)
    return pl.pallas_call(
        conv_kernel,
        in_specs=[pl.BlockSpec(memory_space=pltpu.SMEM)] + [whole] * 3,
        out_specs=whole,
        out_shape=jax.ShapeDtypeStruct((32, 16, 256), bf16),
        scratch_shapes=[
            pltpu.VMEM((640, 512), bf16),
            pltpu.VMEM((512, 256), f32),
            pltpu.VMEM((32, 16, 256), bf16),
            pltpu.VMEM((256, 24, LANES), f32),
            pltpu.VMEM((LANES, 24, LANES), f32),
            pltpu.VMEM((32, 8, LANES), f32),
            pltpu.VMEM((LANES, LANES), f32),
            pltpu.VMEM((LANES, LANES), f32),
        ],
        compiler_params=vmem(24),
        name="conv_rows",
    )(table, recv, taps, skip)


def power_kernel(in_ref, out_ref):
    halves = []
    for half in range(2):
        block = in_ref[:, 8 * half : 8 * half + 8, :].astype(f32).reshape(256, 256)
        halves.append(jnp.sum(block * block, axis=0, keepdims=True))
    line = jnp.concatenate(halves, axis=1)
    for i in range(16):
        out_ref[i] = line


def power_rows(rows):
    return pl.pallas_call(
        power_kernel,
        out_shape=jax.ShapeDtypeStruct((16, 1, 512), f32),
        compiler_params=vmem(4),
        name="power_rows",
    )(rows)


def scale_kernel(in_ref, power_ref, gain_ref, out_ref):
    power = jnp.sum(power_ref[...], axis=0)
    scale = lax.rsqrt(power / 4096.0 + 1e-06)
    gain = gain_ref[...]
    for half in range(2):
        block = in_ref[:, 8 * half : 8 * half + 8, :].astype(f32).reshape(256, 256)
        block = block * scale[:, 256 * half : 256 * half + 256] * gain
        out_ref[256 * half : 256 * half + 256, :] = jnp.transpose(block).astype(bf16)


def scale_rows(rows, power, gain):
    return pl.pallas_call(
        scale_kernel,
        out_shape=jax.ShapeDtypeStruct((512, 256), bf16),
        compiler_params=vmem(4),
        name="scale_rows",
    )(rows, power, gain)


def exchange(block, axis):
    return lax.all_to_all(block, axis, split_axis=0, concat_axis=0, tiled=True)


def local(
    loaded, dest_tiles, tile_counts, segments, short_filters, long_filters, skip_gain, norm_gain
):
    position = lax.axis_index("seq")
    recv = exchange(
        pack(dest_tiles, tile_counts, loaded, long_filters, segments.reshape(4, LANES)), "seq"
    )

    slots = recv[:, 197].astype(jnp.int32)
    placed = (slots[:, 0:32] * 16 + slots[:, 32:64]).reshape(-1)
    tiles = jnp.arange(512, dtype=jnp.int32)
    slot_ids = jnp.arange(1024, dtype=jnp.int32)
    table = jnp.sum(
        jnp.where(placed[None, :] == tiles[:, None], slot_ids[None, :], 0), axis=1
    ).astype(jnp.int32)

    taps = lax.dynamic_slice_in_dim(short_filters, position * 8, 8, 2)
    taps = jnp.broadcast_to(taps[..., None], (3, TAPS, 8, LANES))
    taps = jnp.transpose(taps, (1, 0, 2, 3)).reshape(TAPS, 24, LANES)
    skip = lax.dynamic_slice_in_dim(skip_gain, position * 8, 8, 0)
    skip = jnp.tile(skip, 2)[:, None]

    gated = conv_rows(table, recv, taps, skip)
    mine = exchange(gated, "seq")
    every = exchange(power_rows(mine), "chan")
    return scale_rows(mine, every, norm_gain[:, None])


def solution(mesh):
    return jax.shard_map(
        local,
        mesh=mesh,
        in_specs=(
            P(None, "seq", "chan"),
            P("seq"),
            P("seq"),
            P("seq"),
            P(None, None, "chan"),
            P("chan", "seq"),
            P("chan"),
            P("chan"),
        ),
        out_specs=P("seq", "chan"),
        check_vma=False,
    )
```

```python
import functools

import jax
import jax.numpy as jnp
from jax import lax
from jax.experimental import pallas as pl
from jax.experimental.pallas import tpu as pltpu
from jax.sharding import PartitionSpec as P

TILE = 32
LANES = 128
TAPS = 7
f32 = jnp.float32
bf16 = jnp.bfloat16


def vmem(mib):
    return pltpu.CompilerParams(vmem_limit_bytes=mib << 20)


def turned(block):
    return jnp.transpose(block.astype(f32)).reshape(32, 8, LANES)


def pack_kernel(
    dest_hbm, count_ref, loaded_ref, lags_hbm, segments_hbm, out_ref,
    rows_ref, turned_ref, notes_ref, dest_ref, lags_ref, segments_ref,
    in_sems, out_sems, note_sems,
):
    fetches = []
    small = [
        pltpu.make_async_copy(dest_hbm, dest_ref, note_sems.at[0]),
        pltpu.make_async_copy(lags_hbm, lags_ref, note_sems.at[1]),
        pltpu.make_async_copy(segments_hbm, segments_ref, note_sems.at[2]),
    ]
    for copy in small:
        copy.start()
    for i in range(4):
        fetch = pltpu.make_async_copy(
            loaded_ref.at[:, pl.ds(256 * i, 256), :], rows_ref.at[i], in_sems.at[i]
        )
        fetch.start()
        fetches.append(fetch)

    sends = []
    for i in range(4):
        fetches[i].wait()
        pieces = [
            turned(rows_ref[i, t, LANES * half : LANES * half + LANES, :])
            for t in range(3)
            for half in range(2)
        ]
        turned_ref[i] = jnp.concatenate(pieces, axis=1).astype(bf16)
        send = pltpu.make_async_copy(
            turned_ref.at[i], out_ref.at[:, pl.ds(48 * i, 48), :], out_sems.at[i]
        )
        send.start()
        sends.append(send)
    for copy in small:
        copy.wait()
    lane = lax.broadcasted_iota(jnp.int32, (1, LANES), 1)
    line = jnp.zeros((1, LANES), jnp.int32)
    for j in range(32):
        high = jnp.where(j < count_ref[0], dest_ref[j] >> 4, 63)
        line = jnp.where(lane == j, high, line)
        line = jnp.where(lane == 32 + j, dest_ref[j] & 15, line)
    index = lax.broadcasted_iota(jnp.int32, (LANES, LANES), 0)
    fewer = jnp.zeros((LANES, LANES), f32)
    for j in range(4):
        fewer = fewer + jnp.where(segments_ref[j : j + 1, :] < (index & 63), 1.0, 0.0)
    below = jnp.sum(fewer, axis=1, keepdims=True).astype(jnp.int32)
    below = jnp.where(index[:, :1] < 64, below >> 4, below & 15).astype(f32)
    below = jnp.transpose(jnp.broadcast_to(below, (LANES, LANES)))[:1]
    common = jnp.concatenate([below, line.astype(f32), jnp.zeros((2, LANES), f32)], axis=0)
    lags = lags_ref[...].astype(f32)
    for r in range(16):
        own = [lags[r : r + 1, LANES * j : LANES * j + LANES] for j in range(4)]
        note = jnp.concatenate(own + [common], axis=0).astype(bf16)
        notes_ref[2 * r] = note
        notes_ref[2 * r + 1] = note
    send = pltpu.make_async_copy(notes_ref, out_ref.at[:, pl.ds(192, 8), :], out_sems.at[4])
    send.start()
    sends.append(send)

    for send in sends:
        send.wait()


def pack(dest, count, loaded, lags, segments):
    scalars = pl.BlockSpec(memory_space=pltpu.SMEM)
    far = pl.BlockSpec(memory_space=pltpu.HBM)
    dest, loaded, lags, segments = [
        pltpu.with_memory_space_constraint(a, pltpu.HBM) for a in (dest, loaded, lags, segments)
    ]
    return pl.pallas_call(
        pack_kernel,
        in_specs=[far, scalars, far, far, far],
        out_specs=far,
        out_shape=jax.ShapeDtypeStruct((32, 200, LANES), bf16),
        scratch_shapes=[
            pltpu.VMEM((4, 3, 256, 256), bf16),
            pltpu.VMEM((4, 32, 48, LANES), bf16),
            pltpu.VMEM((32, 8, LANES), bf16),
            pltpu.SMEM((32,), jnp.int32),
            pltpu.VMEM((16, 512), bf16),
            pltpu.VMEM((4, LANES), jnp.int32),
            pltpu.SemaphoreType.DMA((4,)),
            pltpu.SemaphoreType.DMA((5,)),
            pltpu.SemaphoreType.DMA((3,)),
        ],
        compiler_params=vmem(12),
        name="pack",
    )(dest, count, loaded, lags, segments)


def conv_kernel(
    table_ref, recv_ref, taps_ref, skip_ref, out_ref,
    rows_ref, acc_ref, gate_ref, slots_ref, placed_ref, lags_ref, starts_ref, reach_ref,
):
    rows_ref[0:128, :] = jnp.zeros((128, 512), bf16)

    def widen(s, carry):
        for pair in range(4):
            for t in range(3):
                both = recv_ref[s, 48 * pair + 16 * t : 48 * pair + 16 * t + 16, :].astype(f32)
                slots_ref[8 * s + 2 * pair, 8 * t : 8 * t + 8, :] = both[:8]
                slots_ref[8 * s + 2 * pair + 1, 8 * t : 8 * t + 8, :] = both[8:]
        return carry

    lax.fori_loop(0, 32, widen, 0, unroll=2)
    total = jnp.zeros((8, LANES), f32)
    for s in range(32):
        note = recv_ref[s, 192:200, :].astype(f32)
        lags_ref[s] = note
        total = total + note

    starts = 16.0 * total[4:5] + pltpu.roll(total[4:5], 64, 1)
    starts_ref[...] = jnp.transpose(jnp.broadcast_to(starts, (LANES, LANES)))
    row = lax.broadcasted_iota(jnp.int32, (LANES, LANES), 0)
    col = lax.broadcasted_iota(jnp.int32, (LANES, LANES), 1)
    here = (row * LANES + col).astype(f32)

    def latest(v, begin):
        for k in range(8):
            start = jnp.broadcast_to(starts_ref[pl.ds(8 * v + k, 1), :], (LANES, LANES))
            begin = jnp.where(start <= here, start, begin)
        return begin

    begin = lax.fori_loop(0, 8, latest, jnp.zeros((LANES, LANES), f32))
    reach_ref[...] = jnp.minimum(here - begin, 6.0)

    lane = lax.broadcasted_iota(jnp.int32, (24, LANES), 1)
    group = lane // TILE

    def gather(column):
        out = None
        for b in range(4):
            src = table_ref[column * 4 + b]
            tile = pltpu.roll(slots_ref[src >> 2], ((b - src) & 3) * TILE, 1)
            out = tile if out is None else jnp.where(group == b, tile, out)
        placed_ref[column + 1] = out.astype(bf16)

    ahead = lax.broadcasted_iota(jnp.int32, (256, 768), 0)
    lag = lax.broadcasted_iota(jnp.int32, (256, 768), 1)
    shift = (ahead == LANES + (lag & 127) - (lag >> 7) - 1).astype(bf16)

    def short(u, last):
        now = placed_ref[pl.ds(8 * u + 1, 8)]
        both = jnp.concatenate(
            [placed_ref[pl.ds(8 * u, 8)].reshape(192, LANES), now.reshape(192, LANES)], axis=1
        )
        delayed = jnp.dot(both, shift, preferred_element_type=f32)
        for v in range(8 // 4):
            mixed = []
            gates = []
            for k in range(4 * v, 4 * v + 4):
                limit = jnp.broadcast_to(reach_ref[pl.ds(8 * u + k, 1), :], (24, LANES))
                total = now[k].astype(f32) * taps_ref[0]
                for j in range(1, TAPS):
                    part = delayed[24 * k : 24 * k + 24, LANES * (j - 1) : LANES * j]
                    total = total + jnp.where(limit >= j, part, 0.0) * taps_ref[j]
                gates.append(total[:8])
                mixed.append(total[8:16] * total[16:])
            first = jnp.concatenate(mixed[:2], axis=1)
            second = jnp.concatenate(mixed[2:], axis=1)
            at = pl.ds(128 + 32 * u + 16 * v, 16)
            rows_ref[at, 0:256] = jnp.concatenate([first, second], axis=0).astype(bf16)
            rows_ref[at, 256:512] = jnp.concatenate([last, first], axis=0).astype(bf16)
            gate_ref[2 * u + v] = jnp.concatenate(
                [jnp.concatenate(gates[:2], axis=1), jnp.concatenate(gates[2:], axis=1)], axis=0
            ).astype(bf16)
            last = second
        return last

    placed_ref[0] = jnp.zeros((24, LANES), bf16)
    last = jnp.zeros((8, 256), f32)
    for u in range(16):
        for k in range(8):
            gather(8 * u + k)
        last = short(u, last)

    upper = col >= row
    skew = jnp.zeros((LANES, LANES), f32)
    block = jnp.zeros((LANES, LANES), bf16)
    for f in range(0, 32, 2):
        begin = 16 * f
        left, right = [], []
        for g in (f, f + 1):
            at = 128 + begin - 16 * g
            left.append(rows_ref[at : at + 512 - begin, :])
            made = [block]
            for k in range(4):
                line = jnp.broadcast_to(lags_ref[g, k : k + 1, :], (LANES, LANES))
                before, skew = skew, pltpu.roll(line, 0, 1, stride=1, stride_axis=0)
                made.append(jnp.where(upper, skew, before).astype(bf16))
            block = made[4]
            right.append(
                jnp.concatenate(
                    [
                        jnp.concatenate([made[k] for k in (1, 0, 3, 2)], axis=0),
                        jnp.concatenate([made[k] for k in (2, 1, 4, 3)], axis=0),
                    ],
                    axis=1,
                )
            )
        product = jnp.dot(
            jnp.concatenate(left, axis=1),
            jnp.concatenate(right, axis=0),
            preferred_element_type=f32,
        )
        if f == 0:
            acc_ref[...] = product
        else:
            acc_ref[begin:, :] += product

    skip = jnp.broadcast_to(skip_ref[...], (16, 256))

    def finish(u, carry):
        at = pl.ds(pl.multiple_of(16 * u, 16), 16)
        here = pl.ds(pl.multiple_of(128 + 16 * u, 16), 16)
        total = acc_ref[at, :] + skip * rows_ref[here, 0:256].astype(f32)
        out_ref[u] = (gate_ref[u].astype(f32) * total).astype(bf16)
        return carry

    lax.fori_loop(0, 32, finish, 0, unroll=4)


def conv_rows(table, recv, taps, skip):
    whole = pl.BlockSpec(memory_space=pltpu.VMEM)
    return pl.pallas_call(
        conv_kernel,
        in_specs=[pl.BlockSpec(memory_space=pltpu.SMEM)] + [whole] * 3,
        out_specs=whole,
        out_shape=jax.ShapeDtypeStruct((32, 16, 256), bf16),
        scratch_shapes=[
            pltpu.VMEM((640, 512), bf16),
            pltpu.VMEM((512, 256), f32),
            pltpu.VMEM((32, 16, 256), bf16),
            pltpu.VMEM((256, 24, LANES), f32),
            pltpu.VMEM((LANES + 1, 24, LANES), bf16),
            pltpu.VMEM((32, 8, LANES), f32),
            pltpu.VMEM((LANES, LANES), f32),
            pltpu.VMEM((LANES, LANES), f32),
        ],
        compiler_params=vmem(24),
        name="conv_rows",
    )(table, recv, taps, skip)


def power_kernel(in_ref, out_ref):
    halves = []
    for half in range(2):
        block = in_ref[:, 8 * half : 8 * half + 8, :].astype(f32).reshape(256, 256)
        halves.append(jnp.sum(block * block, axis=0, keepdims=True))
    line = jnp.concatenate(halves, axis=1)
    for i in range(16):
        out_ref[i] = line


def power_rows(rows):
    return pl.pallas_call(
        power_kernel,
        out_shape=jax.ShapeDtypeStruct((16, 1, 512), f32),
        compiler_params=vmem(4),
        name="power_rows",
    )(rows)


def scale_kernel(in_ref, power_ref, gain_ref, out_ref):
    power = jnp.sum(power_ref[...], axis=0)
    scale = lax.rsqrt(power / 4096.0 + 1e-06)
    gain = gain_ref[...]
    for half in range(2):
        block = in_ref[:, 8 * half : 8 * half + 8, :].astype(f32).reshape(256, 256)
        block = block * scale[:, 256 * half : 256 * half + 256] * gain
        out_ref[256 * half : 256 * half + 256, :] = jnp.transpose(block).astype(bf16)


def scale_rows(rows, power, gain):
    return pl.pallas_call(
        scale_kernel,
        out_shape=jax.ShapeDtypeStruct((512, 256), bf16),
        compiler_params=vmem(4),
        name="scale_rows",
    )(rows, power, gain)


def exchange(block, axis):
    return lax.all_to_all(block, axis, split_axis=0, concat_axis=0, tiled=True)


def local(
    loaded, dest_tiles, tile_counts, segments, short_filters, long_filters, skip_gain, norm_gain
):
    position = lax.axis_index("seq")
    recv = exchange(
        pack(dest_tiles, tile_counts, loaded, long_filters, segments.reshape(4, LANES)), "seq"
    )

    slots = recv[:, 197].astype(jnp.int32)
    placed = (slots[:, 0:32] * 16 + slots[:, 32:64]).reshape(-1)
    tiles = jnp.arange(512, dtype=jnp.int32)
    slot_ids = jnp.arange(1024, dtype=jnp.int32)
    table = jnp.sum(
        jnp.where(placed[None, :] == tiles[:, None], slot_ids[None, :], 0), axis=1
    ).astype(jnp.int32)

    taps = lax.dynamic_slice_in_dim(short_filters, position * 8, 8, 2)
    taps = jnp.broadcast_to(taps[..., None], (3, TAPS, 8, LANES))
    taps = jnp.transpose(taps, (1, 0, 2, 3)).reshape(TAPS, 24, LANES)
    skip = lax.dynamic_slice_in_dim(skip_gain, position * 8, 8, 0)
    skip = jnp.tile(skip, 2)[:, None]

    gated = conv_rows(table, recv, taps, skip)
    mine = exchange(gated, "seq")
    every = exchange(power_rows(mine), "chan")
    return scale_rows(mine, every, norm_gain[:, None])


def solution(mesh):
    return jax.shard_map(
        local,
        mesh=mesh,
        in_specs=(
            P(None, "seq", "chan"),
            P("seq"),
            P("seq"),
            P("seq"),
            P(None, None, "chan"),
            P("chan", "seq"),
            P("chan"),
            P("chan"),
        ),
        out_specs=P("seq", "chan"),
        check_vma=False,
    )
```

```python
import functools

import jax
import jax.numpy as jnp
from jax import lax
from jax.experimental import pallas as pl
from jax.experimental.pallas import tpu as pltpu
from jax.sharding import PartitionSpec as P

TILE = 32
LANES = 128
TAPS = 7
f32 = jnp.float32
bf16 = jnp.bfloat16


def vmem(mib):
    return pltpu.CompilerParams(vmem_limit_bytes=mib << 20)


def turned(block):
    return jnp.transpose(block.astype(f32)).reshape(32, 8, LANES)


def pack_kernel(
    dest_hbm, count_ref, loaded_ref, lags_hbm, segments_hbm, out_ref,
    rows_ref, dest_ref, lags_ref, segments_ref, in_sems, note_sems,
):
    fetches = []
    small = [
        pltpu.make_async_copy(dest_hbm, dest_ref, note_sems.at[0]),
        pltpu.make_async_copy(lags_hbm, lags_ref, note_sems.at[1]),
        pltpu.make_async_copy(segments_hbm, segments_ref, note_sems.at[2]),
    ]
    for copy in small:
        copy.start()
    for i in range(4):
        fetch = pltpu.make_async_copy(
            loaded_ref.at[:, pl.ds(256 * i, 256), :], rows_ref.at[i], in_sems.at[i]
        )
        fetch.start()
        fetches.append(fetch)

    for i in range(4):
        fetches[i].wait()
        pieces = [
            turned(rows_ref[i, t, LANES * half : LANES * half + LANES, :])
            for t in range(3)
            for half in range(2)
        ]
        out_ref[:, 48 * i : 48 * i + 48, :] = jnp.concatenate(pieces, axis=1).astype(bf16)
    for copy in small:
        copy.wait()
    lane = lax.broadcasted_iota(jnp.int32, (1, LANES), 1)
    line = jnp.zeros((1, LANES), jnp.int32)
    for j in range(32):
        high = jnp.where(j < count_ref[0], dest_ref[j] >> 4, 63)
        line = jnp.where(lane == j, high, line)
        line = jnp.where(lane == 32 + j, dest_ref[j] & 15, line)
    index = lax.broadcasted_iota(jnp.int32, (LANES, LANES), 0)
    fewer = jnp.zeros((LANES, LANES), f32)
    for j in range(4):
        fewer = fewer + jnp.where(segments_ref[j : j + 1, :] < (index & 63), 1.0, 0.0)
    below = jnp.sum(fewer, axis=1, keepdims=True).astype(jnp.int32)
    below = jnp.where(index[:, :1] < 64, below >> 4, below & 15).astype(f32)
    below = jnp.transpose(jnp.broadcast_to(below, (LANES, LANES)))[:1]
    common = jnp.concatenate([below, line.astype(f32), jnp.zeros((2, LANES), f32)], axis=0)
    lags = lags_ref[...].astype(f32)
    for r in range(16):
        own = [lags[r : r + 1, LANES * j : LANES * j + LANES] for j in range(4)]
        note = jnp.concatenate(own + [common], axis=0).astype(bf16)
        out_ref[2 * r, 192:200, :] = note
        out_ref[2 * r + 1, 192:200, :] = note


def pack(dest, count, loaded, lags, segments):
    scalars = pl.BlockSpec(memory_space=pltpu.SMEM)
    far = pl.BlockSpec(memory_space=pltpu.HBM)
    dest, loaded, lags, segments = [
        pltpu.with_memory_space_constraint(a, pltpu.HBM) for a in (dest, loaded, lags, segments)
    ]
    return pl.pallas_call(
        pack_kernel,
        in_specs=[far, scalars, far, far, far],
        out_specs=pl.BlockSpec(memory_space=pltpu.VMEM),
        out_shape=jax.ShapeDtypeStruct((32, 200, LANES), bf16),
        scratch_shapes=[
            pltpu.VMEM((4, 3, 256, 256), bf16),
            pltpu.SMEM((32,), jnp.int32),
            pltpu.VMEM((16, 512), bf16),
            pltpu.VMEM((4, LANES), jnp.int32),
            pltpu.SemaphoreType.DMA((4,)),
            pltpu.SemaphoreType.DMA((3,)),
        ],
        compiler_params=vmem(12),
        name="pack",
    )(dest, count, loaded, lags, segments)


def conv_kernel(
    table_ref, recv_ref, filters_ref, skips_ref, out_ref,
    rows_ref, acc_ref, gate_ref, slots_ref, placed_ref, lags_ref, starts_ref, reach_ref,
    sheet_ref, taps_ref,
):
    rows_ref[0:128, :] = jnp.zeros((128, 512), bf16)

    sheet_ref[16:32, :] = jnp.zeros((16, 256), f32)
    for t in range(3):
        sheet_ref[TAPS * t : TAPS * t + TAPS, :] = filters_ref[t]
    sheet_ref[3 * TAPS : 3 * TAPS + 1, :] = skips_ref[...]
    first_channel = 8 * lax.axis_index("seq")
    sheet = pltpu.roll(sheet_ref[...], (256 - first_channel) & 255, 1)[:, :LANES]
    sheet = jnp.concatenate([sheet, jnp.zeros((96, LANES), f32)], axis=0)
    sheet = jnp.transpose(sheet)[:8]
    for t in range(3):
        for j in range(TAPS):
            value = sheet[:, TAPS * t + j : TAPS * t + j + 1]
            taps_ref[j, 8 * t : 8 * t + 8, :] = jnp.broadcast_to(value, (8, LANES))
    skip = jnp.broadcast_to(sheet[:, 3 * TAPS : 3 * TAPS + 1], (8, 256))
    skip = jnp.concatenate([skip, skip], axis=0)

    def widen(s, carry):
        for pair in range(4):
            for t in range(3):
                both = recv_ref[s, 48 * pair + 16 * t : 48 * pair + 16 * t + 16, :].astype(f32)
                slots_ref[8 * s + 2 * pair, 8 * t : 8 * t + 8, :] = both[:8]
                slots_ref[8 * s + 2 * pair + 1, 8 * t : 8 * t + 8, :] = both[8:]
        return carry

    for s in range(32):
        widen(s, 0)
    total = jnp.zeros((8, LANES), f32)
    for s in range(32):
        note = recv_ref[s, 192:200, :].astype(f32)
        lags_ref[s] = note
        total = total + note

    starts = 16.0 * total[4:5] + pltpu.roll(total[4:5], 64, 1)
    starts_ref[...] = jnp.transpose(jnp.broadcast_to(starts, (LANES, LANES)))
    row = lax.broadcasted_iota(jnp.int32, (LANES, LANES), 0)
    col = lax.broadcasted_iota(jnp.int32, (LANES, LANES), 1)
    here = (row * LANES + col).astype(f32)

    def latest(v, begin):
        for k in range(8):
            start = jnp.broadcast_to(starts_ref[pl.ds(8 * v + k, 1), :], (LANES, LANES))
            begin = jnp.where(start <= here, start, begin)
        return begin

    begin = jnp.zeros((LANES, LANES), f32)
    for v in range(8):
        begin = latest(v, begin)
    reach_ref[...] = jnp.minimum(here - begin, 6.0)

    lane = lax.broadcasted_iota(jnp.int32, (24, LANES), 1)
    group = lane // TILE

    def gather(column):
        out = None
        for b in range(4):
            src = table_ref[column * 4 + b]
            tile = pltpu.roll(slots_ref[src >> 2], ((b - src) & 3) * TILE, 1)
            out = tile if out is None else jnp.where(group == b, tile, out)
        placed_ref[column + 1] = out.astype(bf16)

    ahead = lax.broadcasted_iota(jnp.int32, (256, 768), 0)
    lag = lax.broadcasted_iota(jnp.int32, (256, 768), 1)
    shift = (ahead == LANES + (lag & 127) - (lag >> 7) - 1).astype(bf16)

    def short(u, last):
        now = placed_ref[pl.ds(8 * u + 1, 8)]
        both = jnp.concatenate(
            [placed_ref[pl.ds(8 * u, 8)].reshape(192, LANES), now.reshape(192, LANES)], axis=1
        )
        delayed = jnp.dot(both, shift, preferred_element_type=f32)
        for v in range(8 // 4):
            mixed = []
            gates = []
            for k in range(4 * v, 4 * v + 4):
                limit = jnp.broadcast_to(reach_ref[pl.ds(8 * u + k, 1), :], (24, LANES))
                total = now[k].astype(f32) * taps_ref[0]
                for j in range(1, TAPS):
                    part = delayed[24 * k : 24 * k + 24, LANES * (j - 1) : LANES * j]
                    total = total + jnp.where(limit >= j, part, 0.0) * taps_ref[j]
                gates.append(total[:8])
                mixed.append(total[8:16] * total[16:])
            first = jnp.concatenate(mixed[:2], axis=1)
            second = jnp.concatenate(mixed[2:], axis=1)
            at = pl.ds(128 + 32 * u + 16 * v, 16)
            rows_ref[at, 0:256] = jnp.concatenate([first, second], axis=0).astype(bf16)
            rows_ref[at, 256:512] = jnp.concatenate([last, first], axis=0).astype(bf16)
            gate_ref[2 * u + v] = jnp.concatenate(
                [jnp.concatenate(gates[:2], axis=1), jnp.concatenate(gates[2:], axis=1)], axis=0
            ).astype(bf16)
            last = second
        return last

    placed_ref[0] = jnp.zeros((24, LANES), bf16)
    last = jnp.zeros((8, 256), f32)
    for u in range(16):
        for k in range(8):
            gather(8 * u + k)
        last = short(u, last)

    upper = col >= row
    skew = jnp.zeros((LANES, LANES), f32)
    block = jnp.zeros((LANES, LANES), bf16)
    for f in range(0, 32, 2):
        begin = 16 * f
        left, right = [], []
        for g in (f, f + 1):
            at = 128 + begin - 16 * g
            left.append(rows_ref[at : at + 512 - begin, :])
            made = [block]
            for k in range(4):
                line = jnp.broadcast_to(lags_ref[g, k : k + 1, :], (LANES, LANES))
                before, skew = skew, pltpu.roll(line, 0, 1, stride=1, stride_axis=0)
                made.append(jnp.where(upper, skew, before).astype(bf16))
            block = made[4]
            right.append(
                jnp.concatenate(
                    [
                        jnp.concatenate([made[k] for k in (1, 0, 3, 2)], axis=0),
                        jnp.concatenate([made[k] for k in (2, 1, 4, 3)], axis=0),
                    ],
                    axis=1,
                )
            )
        product = jnp.dot(
            jnp.concatenate(left, axis=1),
            jnp.concatenate(right, axis=0),
            preferred_element_type=f32,
        )
        if f == 0:
            acc_ref[...] = product
        else:
            acc_ref[begin:, :] += product

    def finish(u, carry):
        at = pl.ds(16 * u, 16)
        here = pl.ds(128 + 16 * u, 16)
        total = acc_ref[at, :] + skip * rows_ref[here, 0:256].astype(f32)
        out_ref[u] = (gate_ref[u].astype(f32) * total).astype(bf16)
        return carry

    for u in range(32):
        finish(u, 0)


def conv_rows(table, recv, filters, skips):
    whole = pl.BlockSpec(memory_space=pltpu.VMEM)
    return pl.pallas_call(
        conv_kernel,
        in_specs=[pl.BlockSpec(memory_space=pltpu.SMEM)] + [whole] * 3,
        out_specs=whole,
        out_shape=jax.ShapeDtypeStruct((32, 16, 256), bf16),
        scratch_shapes=[
            pltpu.VMEM((640, 512), bf16),
            pltpu.VMEM((512, 256), f32),
            pltpu.VMEM((32, 16, 256), bf16),
            pltpu.VMEM((256, 24, LANES), f32),
            pltpu.VMEM((LANES + 1, 24, LANES), bf16),
            pltpu.VMEM((32, 8, LANES), f32),
            pltpu.VMEM((LANES, LANES), f32),
            pltpu.VMEM((LANES, LANES), f32),
            pltpu.VMEM((32, 256), f32),
            pltpu.VMEM((TAPS, 24, LANES), f32),
        ],
        compiler_params=vmem(24),
        name="conv_rows",
    )(table, recv, filters, skips)


def power_kernel(in_ref, out_ref):
    halves = []
    for half in range(2):
        block = in_ref[:, 8 * half : 8 * half + 8, :].astype(f32).reshape(256, 256)
        halves.append(jnp.sum(block * block, axis=0, keepdims=True))
    line = jnp.concatenate(halves, axis=1)
    for i in range(16):
        out_ref[i] = line


def power_rows(rows):
    return pl.pallas_call(
        power_kernel,
        out_shape=jax.ShapeDtypeStruct((16, 1, 512), f32),
        compiler_params=vmem(4),
        name="power_rows",
    )(rows)


def scale_kernel(in_ref, power_ref, gain_ref, out_ref):
    power = jnp.sum(power_ref[...], axis=0)
    scale = lax.rsqrt(power / 4096.0 + 1e-06)
    gain = gain_ref[...]
    for half in range(2):
        block = in_ref[:, 8 * half : 8 * half + 8, :].astype(f32).reshape(256, 256)
        block = jnp.transpose(block * scale[:, 256 * half : 256 * half + 256])
        out_ref[256 * half : 256 * half + 256, :] = (block * gain).astype(bf16)


def scale_rows(rows, power, gain):
    return pl.pallas_call(
        scale_kernel,
        out_shape=jax.ShapeDtypeStruct((512, 256), bf16),
        compiler_params=vmem(4),
        name="scale_rows",
    )(rows, power, gain)


def exchange(block, axis):
    return lax.all_to_all(block, axis, split_axis=0, concat_axis=0, tiled=True)


def local(
    loaded, dest_tiles, tile_counts, segments, short_filters, long_filters, skip_gain, norm_gain
):
    recv = exchange(
        pack(dest_tiles, tile_counts, loaded, long_filters, segments.reshape(4, LANES)), "seq"
    )

    slots = recv[:, 197].astype(jnp.int32)
    placed = (slots[:, 0:32] * 16 + slots[:, 32:64]).reshape(-1)
    tiles = jnp.arange(512, dtype=jnp.int32)
    slot_ids = jnp.arange(1024, dtype=jnp.int32)
    table = jnp.sum(
        jnp.where(placed[None, :] == tiles[:, None], slot_ids[None, :], 0), axis=1
    ).astype(jnp.int32)

    gated = conv_rows(table, recv, short_filters, skip_gain.reshape(1, 256))
    mine = exchange(gated, "seq")
    every = exchange(power_rows(mine), "chan")
    return scale_rows(mine, every, norm_gain.reshape(1, 256))


def solution(mesh):
    return jax.shard_map(
        local,
        mesh=mesh,
        in_specs=(
            P(None, "seq", "chan"),
            P("seq"),
            P("seq"),
            P("seq"),
            P(None, None, "chan"),
            P("chan", "seq"),
            P("chan"),
            P("chan"),
        ),
        out_specs=P("seq", "chan"),
        check_vma=False,
    )
```

```python
import functools

import jax
import jax.numpy as jnp
from jax import lax
from jax.experimental import pallas as pl
from jax.experimental.pallas import tpu as pltpu
from jax.sharding import PartitionSpec as P

TILE = 32
LANES = 128
TAPS = 7
f32 = jnp.float32
bf16 = jnp.bfloat16


def vmem(mib):
    return pltpu.CompilerParams(vmem_limit_bytes=mib << 20)


def turned(block):
    return jnp.transpose(block.astype(f32)).reshape(32, 8, LANES)


def pack_kernel(
    dest_hbm, count_ref, loaded_ref, lags_hbm, segments_hbm, out_ref,
    rows_ref, dest_ref, lags_ref, segments_ref, in_sems, note_sems,
):
    fetches = []
    small = [
        pltpu.make_async_copy(dest_hbm, dest_ref, note_sems.at[0]),
        pltpu.make_async_copy(lags_hbm, lags_ref, note_sems.at[1]),
        pltpu.make_async_copy(segments_hbm, segments_ref, note_sems.at[2]),
    ]
    for copy in small:
        copy.start()
    for i in range(4):
        fetch = pltpu.make_async_copy(
            loaded_ref.at[:, pl.ds(256 * i, 256), :], rows_ref.at[i], in_sems.at[i]
        )
        fetch.start()
        fetches.append(fetch)

    for i in range(4):
        fetches[i].wait()
        pieces = [
            turned(rows_ref[i, t, LANES * half : LANES * half + LANES, :])
            for t in range(3)
            for half in range(2)
        ]
        out_ref[:, 48 * i : 48 * i + 48, :] = jnp.concatenate(pieces, axis=1).astype(bf16)
    for copy in small:
        copy.wait()
    lane = lax.broadcasted_iota(jnp.int32, (1, LANES), 1)
    high = jnp.full((1, LANES), 16 * 63, jnp.int32)
    low = jnp.zeros((1, LANES), jnp.int32)
    for j in range(32):
        high = jnp.where((lane == j) & (j < count_ref[0]), dest_ref[j] & 496, high)
        low = jnp.where(lane == j, dest_ref[j] & 15, low)
    index = lax.broadcasted_iota(jnp.int32, (LANES, LANES), 0)
    fewer = jnp.zeros((LANES, LANES), f32)
    for j in range(4):
        fewer = fewer + jnp.where(segments_ref[j : j + 1, :] < (index & 63), 1.0, 0.0)
    below = jnp.sum(fewer, axis=1, keepdims=True).astype(jnp.int32)
    below = jnp.where(index[:, :1] < 64, below >> 4, below & 15).astype(f32)
    below = jnp.transpose(jnp.broadcast_to(below, (LANES, LANES)))[:1]
    common = jnp.concatenate(
        [below, high.astype(f32), low.astype(f32), jnp.zeros((1, LANES), f32)], axis=0
    )
    lags = lags_ref[...].astype(f32)
    for r in range(16):
        own = [lags[r : r + 1, LANES * j : LANES * j + LANES] for j in range(4)]
        note = jnp.concatenate(own + [common], axis=0).astype(bf16)
        out_ref[2 * r, 192:200, :] = note
        out_ref[2 * r + 1, 192:200, :] = note


def pack(dest, count, loaded, lags, segments):
    scalars = pl.BlockSpec(memory_space=pltpu.SMEM)
    far = pl.BlockSpec(memory_space=pltpu.HBM)
    dest, loaded, lags, segments = [
        pltpu.with_memory_space_constraint(a, pltpu.HBM) for a in (dest, loaded, lags, segments)
    ]
    return pl.pallas_call(
        pack_kernel,
        in_specs=[far, scalars, far, far, far],
        out_specs=pl.BlockSpec(memory_space=pltpu.VMEM),
        out_shape=jax.ShapeDtypeStruct((32, 200, LANES), bf16),
        scratch_shapes=[
            pltpu.VMEM((4, 3, 256, 256), bf16),
            pltpu.SMEM((32,), jnp.int32),
            pltpu.VMEM((16, 512), bf16),
            pltpu.VMEM((4, LANES), jnp.int32),
            pltpu.SemaphoreType.DMA((4,)),
            pltpu.SemaphoreType.DMA((3,)),
        ],
        compiler_params=vmem(12),
        name="pack",
    )(dest, count, loaded, lags, segments)


def conv_kernel(
    table_ref, recv_ref, filters_ref, skips_ref, out_ref,
    rows_ref, acc_ref, gate_ref, slots_ref, placed_ref, lags_ref, starts_ref, reach_ref,
    sheet_ref, taps_ref,
):
    rows_ref[0:128, :] = jnp.zeros((128, 512), bf16)

    sheet_ref[16:32, :] = jnp.zeros((16, 256), f32)
    for t in range(3):
        sheet_ref[TAPS * t : TAPS * t + TAPS, :] = filters_ref[t]
    sheet_ref[3 * TAPS : 3 * TAPS + 1, :] = skips_ref[...]
    first_channel = 8 * lax.axis_index("seq")
    sheet = pltpu.roll(sheet_ref[...], (256 - first_channel) & 255, 1)[:, :LANES]
    sheet = jnp.concatenate([sheet, jnp.zeros((96, LANES), f32)], axis=0)
    sheet = jnp.transpose(sheet)[:8]
    for t in range(3):
        for j in range(TAPS):
            value = sheet[:, TAPS * t + j : TAPS * t + j + 1]
            taps_ref[j, 8 * t : 8 * t + 8, :] = jnp.broadcast_to(value, (8, LANES))
    skip = jnp.broadcast_to(sheet[:, 3 * TAPS : 3 * TAPS + 1], (8, 256))
    skip = jnp.concatenate([skip, skip], axis=0)

    def widen(s, carry):
        for pair in range(4):
            for t in range(3):
                both = recv_ref[s, 48 * pair + 16 * t : 48 * pair + 16 * t + 16, :].astype(f32)
                slots_ref[8 * s + 2 * pair, 8 * t : 8 * t + 8, :] = both[:8]
                slots_ref[8 * s + 2 * pair + 1, 8 * t : 8 * t + 8, :] = both[8:]
        return carry

    for s in range(32):
        widen(s, 0)
    total = jnp.zeros((8, LANES), f32)
    for s in range(32):
        note = recv_ref[s, 192:200, :].astype(f32)
        lags_ref[s] = note
        total = total + note

    starts = 16.0 * total[4:5] + pltpu.roll(total[4:5], 64, 1)
    starts_ref[...] = jnp.transpose(jnp.broadcast_to(starts, (LANES, LANES)))
    row = lax.broadcasted_iota(jnp.int32, (LANES, LANES), 0)
    col = lax.broadcasted_iota(jnp.int32, (LANES, LANES), 1)
    here = (row * LANES + col).astype(f32)

    def latest(v, begin):
        for k in range(8):
            start = jnp.broadcast_to(starts_ref[pl.ds(8 * v + k, 1), :], (LANES, LANES))
            begin = jnp.where(start <= here, start, begin)
        return begin

    begin = jnp.zeros((LANES, LANES), f32)
    for v in range(8):
        begin = latest(v, begin)
    reach_ref[...] = jnp.minimum(here - begin, 6.0)

    lane = lax.broadcasted_iota(jnp.int32, (24, LANES), 1)
    group = lane // TILE

    def gather(column):
        out = None
        for b in range(4):
            src = table_ref[column * 4 + b]
            tile = pltpu.roll(slots_ref[src >> 2], ((b - src) & 3) * TILE, 1)
            out = tile if out is None else jnp.where(group == b, tile, out)
        placed_ref[column + 1] = out.astype(bf16)

    ahead = lax.broadcasted_iota(jnp.int32, (256, 768), 0)
    lag = lax.broadcasted_iota(jnp.int32, (256, 768), 1)
    shift = (ahead == LANES + (lag & 127) - (lag >> 7) - 1).astype(bf16)

    def short(u, last):
        now = placed_ref[pl.ds(8 * u + 1, 8)]
        both = jnp.concatenate(
            [placed_ref[pl.ds(8 * u, 8)].reshape(192, LANES), now.reshape(192, LANES)], axis=1
        )
        delayed = jnp.dot(both, shift, preferred_element_type=f32)
        for v in range(8 // 4):
            mixed = []
            gates = []
            for k in range(4 * v, 4 * v + 4):
                limit = jnp.broadcast_to(reach_ref[pl.ds(8 * u + k, 1), :], (24, LANES))
                total = now[k].astype(f32) * taps_ref[0]
                for j in range(1, TAPS):
                    part = delayed[24 * k : 24 * k + 24, LANES * (j - 1) : LANES * j]
                    total = total + jnp.where(limit >= j, part, 0.0) * taps_ref[j]
                gates.append(total[:8])
                mixed.append(total[8:16] * total[16:])
            first = jnp.concatenate(mixed[:2], axis=1)
            second = jnp.concatenate(mixed[2:], axis=1)
            at = pl.ds(128 + 32 * u + 16 * v, 16)
            rows_ref[at, 0:256] = jnp.concatenate([first, second], axis=0).astype(bf16)
            rows_ref[at, 256:512] = jnp.concatenate([last, first], axis=0).astype(bf16)
            gate_ref[2 * u + v] = jnp.concatenate(
                [jnp.concatenate(gates[:2], axis=1), jnp.concatenate(gates[2:], axis=1)], axis=0
            ).astype(bf16)
            last = second
        return last

    placed_ref[0] = jnp.zeros((24, LANES), bf16)
    last = jnp.zeros((8, 256), f32)
    for u in range(16):
        for k in range(8):
            gather(8 * u + k)
        last = short(u, last)

    upper = col >= row
    skew = jnp.zeros((LANES, LANES), f32)
    block = jnp.zeros((LANES, LANES), bf16)
    for f in range(0, 32, 2):
        begin = 16 * f
        left, right = [], []
        for g in (f, f + 1):
            at = 128 + begin - 16 * g
            left.append(rows_ref[at : at + 512 - begin, :])
            made = [block]
            for k in range(4):
                line = jnp.broadcast_to(lags_ref[g, k : k + 1, :], (LANES, LANES))
                before, skew = skew, pltpu.roll(line, 0, 1, stride=1, stride_axis=0)
                made.append(jnp.where(upper, skew, before).astype(bf16))
            block = made[4]
            right.append(
                jnp.concatenate(
                    [
                        jnp.concatenate([made[k] for k in (1, 0, 3, 2)], axis=0),
                        jnp.concatenate([made[k] for k in (2, 1, 4, 3)], axis=0),
                    ],
                    axis=1,
                )
            )
        product = jnp.dot(
            jnp.concatenate(left, axis=1),
            jnp.concatenate(right, axis=0),
            preferred_element_type=f32,
        )
        if f == 0:
            acc_ref[...] = product
        else:
            acc_ref[begin:, :] += product

    def finish(u, carry):
        at = pl.ds(16 * u, 16)
        here = pl.ds(128 + 16 * u, 16)
        total = acc_ref[at, :] + skip * rows_ref[here, 0:256].astype(f32)
        out_ref[u] = (gate_ref[u].astype(f32) * total).astype(bf16)
        return carry

    for u in range(32):
        finish(u, 0)


def conv_rows(table, recv, filters, skips):
    whole = pl.BlockSpec(memory_space=pltpu.VMEM)
    return pl.pallas_call(
        conv_kernel,
        in_specs=[pl.BlockSpec(memory_space=pltpu.SMEM)] + [whole] * 3,
        out_specs=whole,
        out_shape=jax.ShapeDtypeStruct((32, 16, 256), bf16),
        scratch_shapes=[
            pltpu.VMEM((640, 512), bf16),
            pltpu.VMEM((512, 256), f32),
            pltpu.VMEM((32, 16, 256), bf16),
            pltpu.VMEM((256, 24, LANES), f32),
            pltpu.VMEM((LANES + 1, 24, LANES), bf16),
            pltpu.VMEM((32, 8, LANES), f32),
            pltpu.VMEM((LANES, LANES), f32),
            pltpu.VMEM((LANES, LANES), f32),
            pltpu.VMEM((32, 256), f32),
            pltpu.VMEM((TAPS, 24, LANES), f32),
        ],
        compiler_params=vmem(24),
        name="conv_rows",
    )(table, recv, filters, skips)


def power_kernel(in_ref, out_ref):
    halves = []
    for half in range(2):
        block = in_ref[:, 8 * half : 8 * half + 8, :].astype(f32).reshape(256, 256)
        halves.append(jnp.sum(block * block, axis=0, keepdims=True))
    line = jnp.concatenate(halves, axis=1)
    for i in range(16):
        out_ref[i] = line


def power_rows(rows):
    return pl.pallas_call(
        power_kernel,
        out_shape=jax.ShapeDtypeStruct((16, 1, 512), f32),
        compiler_params=vmem(4),
        name="power_rows",
    )(rows)


def scale_kernel(in_ref, power_ref, gain_ref, out_ref):
    power = jnp.sum(power_ref[...], axis=0)
    scale = lax.rsqrt(power / 4096.0 + 1e-06)
    gain = gain_ref[...]
    for half in range(2):
        block = in_ref[:, 8 * half : 8 * half + 8, :].astype(f32).reshape(256, 256)
        block = jnp.transpose(block * scale[:, 256 * half : 256 * half + 256])
        out_ref[256 * half : 256 * half + 256, :] = (block * gain).astype(bf16)


def scale_rows(rows, power, gain):
    return pl.pallas_call(
        scale_kernel,
        out_shape=jax.ShapeDtypeStruct((512, 256), bf16),
        compiler_params=vmem(4),
        name="scale_rows",
    )(rows, power, gain)


def exchange(block, axis):
    return lax.all_to_all(block, axis, split_axis=0, concat_axis=0, tiled=True)


def local(
    loaded, dest_tiles, tile_counts, segments, short_filters, long_filters, skip_gain, norm_gain
):
    recv = exchange(
        pack(dest_tiles, tile_counts, loaded, long_filters, segments.reshape(4, LANES)), "seq"
    )

    placed = (recv[:, 197, :32].astype(f32) + recv[:, 198, :32].astype(f32)).astype(jnp.int32)
    placed = placed.reshape(-1)
    tiles = jnp.arange(512, dtype=jnp.int32)
    slot_ids = jnp.arange(1024, dtype=jnp.int32)
    table = jnp.sum(
        jnp.where(placed[None, :] == tiles[:, None], slot_ids[None, :], 0), axis=1
    ).astype(jnp.int32)

    gated = conv_rows(table, recv, short_filters, skip_gain.reshape(1, 256))
    mine = exchange(gated, "seq")
    every = exchange(power_rows(mine), "chan")
    return scale_rows(mine, every, norm_gain.reshape(1, 256))


def solution(mesh):
    return jax.shard_map(
        local,
        mesh=mesh,
        in_specs=(
            P(None, "seq", "chan"),
            P("seq"),
            P("seq"),
            P("seq"),
            P(None, None, "chan"),
            P("chan", "seq"),
            P("chan"),
            P("chan"),
        ),
        out_specs=P("seq", "chan"),
        check_vma=False,
    )
```

```python
import functools

import jax
import jax.numpy as jnp
from jax import lax
from jax.experimental import pallas as pl
from jax.experimental.pallas import tpu as pltpu
from jax.sharding import PartitionSpec as P

TILE = 32
LANES = 128
TAPS = 7
f32 = jnp.float32
bf16 = jnp.bfloat16


def vmem(mib):
    return pltpu.CompilerParams(vmem_limit_bytes=mib << 20)


def turned(block):
    return jnp.transpose(block.astype(f32)).reshape(32, 8, LANES)


def pack_kernel(
    dest_hbm, count_ref, loaded_ref, lags_hbm, segments_hbm, out_ref,
    rows_ref, dest_ref, lags_ref, segments_ref, in_sems, note_sems,
):
    fetches = []
    small = [
        pltpu.make_async_copy(dest_hbm, dest_ref, note_sems.at[0]),
        pltpu.make_async_copy(lags_hbm, lags_ref, note_sems.at[1]),
        pltpu.make_async_copy(segments_hbm, segments_ref, note_sems.at[2]),
    ]
    for copy in small:
        copy.start()
    for i in range(4):
        fetch = pltpu.make_async_copy(
            loaded_ref.at[:, pl.ds(256 * i, 256), :], rows_ref.at[i], in_sems.at[i]
        )
        fetch.start()
        fetches.append(fetch)

    for i in range(4):
        fetches[i].wait()
        pieces = [
            turned(rows_ref[i, t, LANES * half : LANES * half + LANES, :])
            for t in range(3)
            for half in range(2)
        ]
        out_ref[:, 48 * i : 48 * i + 48, :] = jnp.concatenate(pieces, axis=1).astype(bf16)
    for copy in small:
        copy.wait()
    lane = lax.broadcasted_iota(jnp.int32, (1, LANES), 1)
    high = jnp.full((1, LANES), 16 * 63, jnp.int32)
    low = jnp.zeros((1, LANES), jnp.int32)
    for j in range(32):
        high = jnp.where((lane == j) & (j < count_ref[0]), dest_ref[j] & 496, high)
        low = jnp.where(lane == j, dest_ref[j] & 15, low)
    index = lax.broadcasted_iota(jnp.int32, (LANES, LANES), 0)
    fewer = jnp.zeros((LANES, LANES), f32)
    for j in range(4):
        fewer = fewer + jnp.where(segments_ref[j : j + 1, :] < (index & 63), 1.0, 0.0)
    below = jnp.sum(fewer, axis=1, keepdims=True).astype(jnp.int32)
    below = jnp.where(index[:, :1] < 64, below >> 4, below & 15).astype(f32)
    below = jnp.transpose(jnp.broadcast_to(below, (LANES, LANES)))[:1]
    common = jnp.concatenate(
        [below, high.astype(f32), low.astype(f32), jnp.zeros((1, LANES), f32)], axis=0
    )
    lags = lags_ref[...].astype(f32)
    for r in range(16):
        own = [lags[r : r + 1, LANES * j : LANES * j + LANES] for j in range(4)]
        note = jnp.concatenate(own + [common], axis=0).astype(bf16)
        out_ref[2 * r, 192:200, :] = note
        out_ref[2 * r + 1, 192:200, :] = note


def pack(dest, count, loaded, lags, segments):
    scalars = pl.BlockSpec(memory_space=pltpu.SMEM)
    far = pl.BlockSpec(memory_space=pltpu.HBM)
    dest, loaded, lags, segments = [
        pltpu.with_memory_space_constraint(a, pltpu.HBM) for a in (dest, loaded, lags, segments)
    ]
    return pl.pallas_call(
        pack_kernel,
        in_specs=[far, scalars, far, far, far],
        out_specs=pl.BlockSpec(memory_space=pltpu.VMEM),
        out_shape=jax.ShapeDtypeStruct((32, 200, LANES), bf16),
        scratch_shapes=[
            pltpu.VMEM((4, 3, 256, 256), bf16),
            pltpu.SMEM((32,), jnp.int32),
            pltpu.VMEM((16, 512), bf16),
            pltpu.VMEM((4, LANES), jnp.int32),
            pltpu.SemaphoreType.DMA((4,)),
            pltpu.SemaphoreType.DMA((3,)),
        ],
        compiler_params=vmem(12),
        name="pack",
    )(dest, count, loaded, lags, segments)


def conv_kernel(
    table_ref, recv_ref, filters_ref, skips_ref, out_ref,
    rows_ref, acc_ref, gate_ref, slots_ref, placed_ref, lags_ref, starts_ref, reach_ref,
    sheet_ref, taps_ref,
):
    rows_ref[0:128, :] = jnp.zeros((128, 512), bf16)

    sheet_ref[16:32, :] = jnp.zeros((16, 256), f32)
    for t in range(3):
        sheet_ref[TAPS * t : TAPS * t + TAPS, :] = filters_ref[t]
    sheet_ref[3 * TAPS : 3 * TAPS + 1, :] = skips_ref[...]
    first_channel = 8 * lax.axis_index("seq")
    sheet = pltpu.roll(sheet_ref[...], (256 - first_channel) & 255, 1)[:, :LANES]
    sheet = jnp.concatenate([sheet, jnp.zeros((96, LANES), f32)], axis=0)
    sheet = jnp.transpose(sheet)[:8]
    for t in range(3):
        for j in range(TAPS):
            value = sheet[:, TAPS * t + j : TAPS * t + j + 1]
            taps_ref[j, 8 * t : 8 * t + 8, :] = jnp.broadcast_to(value, (8, LANES))
    skip = jnp.broadcast_to(sheet[:, 3 * TAPS : 3 * TAPS + 1], (8, 256))
    skip = jnp.concatenate([skip, skip], axis=0)

    def widen(s, carry):
        for pair in range(4):
            for t in range(3):
                both = recv_ref[s, 48 * pair + 16 * t : 48 * pair + 16 * t + 16, :].astype(f32)
                slots_ref[8 * s + 2 * pair, 8 * t : 8 * t + 8, :] = both[:8]
                slots_ref[8 * s + 2 * pair + 1, 8 * t : 8 * t + 8, :] = both[8:]
        return carry

    for s in range(32):
        widen(s, 0)
    total = jnp.zeros((8, LANES), f32)
    for s in range(32):
        note = recv_ref[s, 192:200, :].astype(f32)
        lags_ref[s] = note
        total = total + note

    starts = 16.0 * total[4:5] + pltpu.roll(total[4:5], 64, 1)
    starts_ref[...] = jnp.transpose(jnp.broadcast_to(starts, (LANES, LANES)))
    row = lax.broadcasted_iota(jnp.int32, (LANES, LANES), 0)
    col = lax.broadcasted_iota(jnp.int32, (LANES, LANES), 1)
    here = (row * LANES + col).astype(f32)

    def latest(v, begin):
        for k in range(8):
            start = jnp.broadcast_to(starts_ref[pl.ds(8 * v + k, 1), :], (LANES, LANES))
            begin = jnp.where(start <= here, start, begin)
        return begin

    begin = jnp.zeros((LANES, LANES), f32)
    for v in range(8):
        begin = latest(v, begin)
    reach_ref[...] = jnp.minimum(here - begin, 6.0)

    lane = lax.broadcasted_iota(jnp.int32, (24, LANES), 1)
    group = lane // TILE

    def gather(column):
        out = None
        for b in range(4):
            src = table_ref[column * 4 + b]
            tile = pltpu.roll(slots_ref[src >> 2], ((b - src) & 3) * TILE, 1)
            out = tile if out is None else jnp.where(group == b, tile, out)
        placed_ref[column + 1] = out.astype(bf16)

    ahead = lax.broadcasted_iota(jnp.int32, (256, 768), 0)
    lag = lax.broadcasted_iota(jnp.int32, (256, 768), 1)
    shift = (ahead == LANES + (lag & 127) - (lag >> 7) - 1).astype(bf16)

    def short(u, last):
        now = placed_ref[pl.ds(16 * u + 1, 16)]
        both = jnp.concatenate(
            [placed_ref[pl.ds(16 * u, 16)].reshape(384, LANES), now.reshape(384, LANES)], axis=1
        )
        delayed = jnp.dot(both, shift, preferred_element_type=f32)
        for v in range(16 // 4):
            mixed = []
            gates = []
            for k in range(4 * v, 4 * v + 4):
                limit = jnp.broadcast_to(reach_ref[pl.ds(16 * u + k, 1), :], (24, LANES))
                total = now[k].astype(f32) * taps_ref[0]
                for j in range(1, TAPS):
                    part = delayed[24 * k : 24 * k + 24, LANES * (j - 1) : LANES * j]
                    total = total + jnp.where(limit >= j, part, 0.0) * taps_ref[j]
                gates.append(total[:8])
                mixed.append(total[8:16] * total[16:])
            first = jnp.concatenate(mixed[:2], axis=1)
            second = jnp.concatenate(mixed[2:], axis=1)
            at = pl.ds(128 + 64 * u + 16 * v, 16)
            rows_ref[at, 0:256] = jnp.concatenate([first, second], axis=0).astype(bf16)
            rows_ref[at, 256:512] = jnp.concatenate([last, first], axis=0).astype(bf16)
            gate_ref[4 * u + v] = jnp.concatenate(
                [jnp.concatenate(gates[:2], axis=1), jnp.concatenate(gates[2:], axis=1)], axis=0
            ).astype(bf16)
            last = second
        return last

    placed_ref[0] = jnp.zeros((24, LANES), bf16)
    last = jnp.zeros((8, 256), f32)
    for u in range(8):
        for k in range(16):
            gather(16 * u + k)
        last = short(u, last)

    upper = col >= row
    skew = jnp.zeros((LANES, LANES), f32)
    block = jnp.zeros((LANES, LANES), bf16)
    for f in range(0, 32, 2):
        begin = 16 * f
        left, right = [], []
        for g in (f, f + 1):
            at = 128 + begin - 16 * g
            left.append(rows_ref[at : at + 512 - begin, :])
            made = [block]
            for k in range(4):
                line = jnp.broadcast_to(lags_ref[g, k : k + 1, :], (LANES, LANES))
                before, skew = skew, pltpu.roll(line, 0, 1, stride=1, stride_axis=0)
                made.append(jnp.where(upper, skew, before).astype(bf16))
            block = made[4]
            right.append(
                jnp.concatenate(
                    [
                        jnp.concatenate([made[k] for k in (1, 0, 3, 2)], axis=0),
                        jnp.concatenate([made[k] for k in (2, 1, 4, 3)], axis=0),
                    ],
                    axis=1,
                )
            )
        product = jnp.dot(
            jnp.concatenate(left, axis=1),
            jnp.concatenate(right, axis=0),
            preferred_element_type=f32,
        )
        if f == 0:
            acc_ref[...] = product
        else:
            acc_ref[begin:, :] += product

    def finish(u, carry):
        at = pl.ds(16 * u, 16)
        here = pl.ds(128 + 16 * u, 16)
        total = acc_ref[at, :] + skip * rows_ref[here, 0:256].astype(f32)
        out_ref[u] = (gate_ref[u].astype(f32) * total).astype(bf16)
        return carry

    for u in range(32):
        finish(u, 0)


def conv_rows(table, recv, filters, skips):
    whole = pl.BlockSpec(memory_space=pltpu.VMEM)
    return pl.pallas_call(
        conv_kernel,
        in_specs=[pl.BlockSpec(memory_space=pltpu.SMEM)] + [whole] * 3,
        out_specs=whole,
        out_shape=jax.ShapeDtypeStruct((32, 16, 256), bf16),
        scratch_shapes=[
            pltpu.VMEM((640, 512), bf16),
            pltpu.VMEM((512, 256), f32),
            pltpu.VMEM((32, 16, 256), bf16),
            pltpu.VMEM((256, 24, LANES), f32),
            pltpu.VMEM((LANES + 1, 24, LANES), bf16),
            pltpu.VMEM((32, 8, LANES), f32),
            pltpu.VMEM((LANES, LANES), f32),
            pltpu.VMEM((LANES, LANES), f32),
            pltpu.VMEM((32, 256), f32),
            pltpu.VMEM((TAPS, 24, LANES), f32),
        ],
        compiler_params=vmem(24),
        name="conv_rows",
    )(table, recv, filters, skips)


def power_kernel(in_ref, out_ref):
    halves = []
    for half in range(2):
        block = in_ref[:, 8 * half : 8 * half + 8, :].astype(f32).reshape(256, 256)
        halves.append(jnp.sum(block * block, axis=0, keepdims=True))
    line = jnp.concatenate(halves, axis=1)
    for i in range(16):
        out_ref[i] = line


def power_rows(rows):
    return pl.pallas_call(
        power_kernel,
        out_shape=jax.ShapeDtypeStruct((16, 1, 512), f32),
        compiler_params=vmem(4),
        name="power_rows",
    )(rows)


def scale_kernel(in_ref, power_ref, gain_ref, out_ref):
    power = jnp.sum(power_ref[...], axis=0)
    scale = lax.rsqrt(power / 4096.0 + 1e-06)
    gain = gain_ref[...]
    for half in range(2):
        block = in_ref[:, 8 * half : 8 * half + 8, :].astype(f32).reshape(256, 256)
        block = jnp.transpose(block * scale[:, 256 * half : 256 * half + 256])
        out_ref[256 * half : 256 * half + 256, :] = (block * gain).astype(bf16)


def scale_rows(rows, power, gain):
    return pl.pallas_call(
        scale_kernel,
        out_shape=jax.ShapeDtypeStruct((512, 256), bf16),
        compiler_params=vmem(4),
        name="scale_rows",
    )(rows, power, gain)


def exchange(block, axis):
    return lax.all_to_all(block, axis, split_axis=0, concat_axis=0, tiled=True)


def local(
    loaded, dest_tiles, tile_counts, segments, short_filters, long_filters, skip_gain, norm_gain
):
    recv = exchange(
        pack(dest_tiles, tile_counts, loaded, long_filters, segments.reshape(4, LANES)), "seq"
    )

    placed = (recv[:, 197, :32].astype(f32) + recv[:, 198, :32].astype(f32)).astype(jnp.int32)
    placed = placed.reshape(-1)
    tiles = jnp.arange(512, dtype=jnp.int32)
    slot_ids = jnp.arange(1024, dtype=jnp.int32)
    table = jnp.sum(
        jnp.where(placed[None, :] == tiles[:, None], slot_ids[None, :], 0), axis=1
    ).astype(jnp.int32)

    gated = conv_rows(table, recv, short_filters, skip_gain.reshape(1, 256))
    mine = exchange(gated, "seq")
    every = exchange(power_rows(mine), "chan")
    return scale_rows(mine, every, norm_gain.reshape(1, 256))


def solution(mesh):
    return jax.shard_map(
        local,
        mesh=mesh,
        in_specs=(
            P(None, "seq", "chan"),
            P("seq"),
            P("seq"),
            P("seq"),
            P(None, None, "chan"),
            P("chan", "seq"),
            P("chan"),
            P("chan"),
        ),
        out_specs=P("seq", "chan"),
        check_vma=False,
    )
```

```python
import functools

import jax
import jax.numpy as jnp
from jax import lax
from jax.experimental import pallas as pl
from jax.experimental.pallas import tpu as pltpu
from jax.sharding import PartitionSpec as P

TILE = 32
LANES = 128
TAPS = 7
f32 = jnp.float32
bf16 = jnp.bfloat16


def vmem(mib):
    return pltpu.CompilerParams(vmem_limit_bytes=mib << 20)


def turned(block):
    return jnp.transpose(block.astype(f32)).reshape(32, 8, LANES)


def pack_kernel(
    dest_hbm, count_ref, loaded_ref, lags_hbm, segments_hbm, out_ref,
    rows_ref, dest_ref, lags_ref, segments_ref, in_sems, note_sems,
):
    fetches = []
    small = [
        pltpu.make_async_copy(dest_hbm, dest_ref, note_sems.at[0]),
        pltpu.make_async_copy(lags_hbm, lags_ref, note_sems.at[1]),
        pltpu.make_async_copy(segments_hbm, segments_ref, note_sems.at[2]),
    ]
    for copy in small:
        copy.start()
    for i in range(4):
        fetch = pltpu.make_async_copy(
            loaded_ref.at[:, pl.ds(256 * i, 256), :], rows_ref.at[i], in_sems.at[i]
        )
        fetch.start()
        fetches.append(fetch)

    for i in range(4):
        fetches[i].wait()
        pieces = [
            turned(rows_ref[i, t, LANES * half : LANES * half + LANES, :])
            for t in range(3)
            for half in range(2)
        ]
        out_ref[:, 48 * i : 48 * i + 48, :] = jnp.concatenate(pieces, axis=1).astype(bf16)
    for copy in small:
        copy.wait()
    lane = lax.broadcasted_iota(jnp.int32, (1, LANES), 1)
    high = jnp.full((1, LANES), 16 * 63, jnp.int32)
    low = jnp.zeros((1, LANES), jnp.int32)
    for j in range(32):
        high = jnp.where((lane == j) & (j < count_ref[0]), dest_ref[j] & 496, high)
        low = jnp.where(lane == j, dest_ref[j] & 15, low)
    index = lax.broadcasted_iota(jnp.int32, (LANES, LANES), 0)
    fewer = jnp.zeros((LANES, LANES), f32)
    for j in range(4):
        fewer = fewer + jnp.where(segments_ref[j : j + 1, :] < (index & 63), 1.0, 0.0)
    below = jnp.sum(fewer, axis=1, keepdims=True).astype(jnp.int32)
    below = jnp.where(index[:, :1] < 64, below >> 4, below & 15).astype(f32)
    below = jnp.transpose(jnp.broadcast_to(below, (LANES, LANES)))[:1]
    common = jnp.concatenate(
        [below, high.astype(f32), low.astype(f32), jnp.zeros((1, LANES), f32)], axis=0
    )
    lags = lags_ref[...].astype(f32)
    for r in range(16):
        own = [lags[r : r + 1, LANES * j : LANES * j + LANES] for j in range(4)]
        note = jnp.concatenate(own + [common], axis=0).astype(bf16)
        out_ref[2 * r, 192:200, :] = note
        out_ref[2 * r + 1, 192:200, :] = note


def pack(dest, count, loaded, lags, segments):
    scalars = pl.BlockSpec(memory_space=pltpu.SMEM)
    far = pl.BlockSpec(memory_space=pltpu.HBM)
    dest, loaded, lags, segments = [
        pltpu.with_memory_space_constraint(a, pltpu.HBM) for a in (dest, loaded, lags, segments)
    ]
    return pl.pallas_call(
        pack_kernel,
        in_specs=[far, scalars, far, far, far],
        out_specs=pl.BlockSpec(memory_space=pltpu.VMEM),
        out_shape=jax.ShapeDtypeStruct((32, 200, LANES), bf16),
        scratch_shapes=[
            pltpu.VMEM((4, 3, 256, 256), bf16),
            pltpu.SMEM((32,), jnp.int32),
            pltpu.VMEM((16, 512), bf16),
            pltpu.VMEM((4, LANES), jnp.int32),
            pltpu.SemaphoreType.DMA((4,)),
            pltpu.SemaphoreType.DMA((3,)),
        ],
        compiler_params=vmem(12),
        name="pack",
    )(dest, count, loaded, lags, segments)


def conv_kernel(
    table_ref, recv_ref, filters_ref, skips_ref, out_ref,
    rows_ref, acc_ref, gate_ref, slots_ref, placed_ref, lags_ref, starts_ref, reach_ref,
    sheet_ref, taps_ref,
):
    rows_ref[0:128, :] = jnp.zeros((128, 512), bf16)

    sheet_ref[16:32, :] = jnp.zeros((16, 256), f32)
    for t in range(3):
        sheet_ref[TAPS * t : TAPS * t + TAPS, :] = filters_ref[t]
    sheet_ref[3 * TAPS : 3 * TAPS + 1, :] = skips_ref[...]
    first_channel = 8 * lax.axis_index("seq")
    sheet = pltpu.roll(sheet_ref[...], (256 - first_channel) & 255, 1)[:, :LANES]
    sheet = jnp.concatenate([sheet, jnp.zeros((96, LANES), f32)], axis=0)
    sheet = jnp.transpose(sheet)[:8]
    for t in range(3):
        for j in range(TAPS):
            value = sheet[:, TAPS * t + j : TAPS * t + j + 1]
            taps_ref[j, 8 * t : 8 * t + 8, :] = jnp.broadcast_to(value, (8, LANES))
    skip = jnp.broadcast_to(sheet[:, 3 * TAPS : 3 * TAPS + 1], (8, 256))
    skip = jnp.concatenate([skip, skip], axis=0)

    def widen(s, carry):
        for pair in range(4):
            for t in range(3):
                both = recv_ref[s, 48 * pair + 16 * t : 48 * pair + 16 * t + 16, :].astype(f32)
                slots_ref[8 * s + 2 * pair, 8 * t : 8 * t + 8, :] = both[:8]
                slots_ref[8 * s + 2 * pair + 1, 8 * t : 8 * t + 8, :] = both[8:]
        return carry

    for s in range(32):
        widen(s, 0)
    total = jnp.zeros((8, LANES), f32)
    for s in range(32):
        note = recv_ref[s, 192:200, :].astype(f32)
        lags_ref[s] = note
        total = total + note

    starts = 16.0 * total[4:5] + pltpu.roll(total[4:5], 64, 1)
    starts_ref[...] = jnp.transpose(jnp.broadcast_to(starts, (LANES, LANES)))
    row = lax.broadcasted_iota(jnp.int32, (LANES, LANES), 0)
    col = lax.broadcasted_iota(jnp.int32, (LANES, LANES), 1)
    here = (row * LANES + col).astype(f32)

    def latest(v, begin):
        for k in range(8):
            start = jnp.broadcast_to(starts_ref[pl.ds(8 * v + k, 1), :], (LANES, LANES))
            begin = jnp.where(start <= here, start, begin)
        return begin

    begin = jnp.zeros((LANES, LANES), f32)
    for v in range(8):
        begin = latest(v, begin)
    reach_ref[...] = jnp.minimum(here - begin, 6.0)

    lane = lax.broadcasted_iota(jnp.int32, (24, LANES), 1)
    group = lane // TILE

    def gather(column):
        out = None
        for b in range(4):
            src = table_ref[column * 4 + b]
            tile = pltpu.roll(slots_ref[src >> 2], ((b - src) & 3) * TILE, 1)
            out = tile if out is None else jnp.where(group == b, tile, out)
        placed_ref[column + 1] = out.astype(bf16)

    ahead = lax.broadcasted_iota(jnp.int32, (256, 768), 0)
    lag = lax.broadcasted_iota(jnp.int32, (256, 768), 1)
    shift = (ahead == LANES + (lag & 127) - (lag >> 7) - 1).astype(bf16)

    def short(u, last):
        now = placed_ref[pl.ds(8 * u + 1, 8)]
        both = jnp.concatenate(
            [placed_ref[pl.ds(8 * u, 8)].reshape(192, LANES), now.reshape(192, LANES)], axis=1
        )
        delayed = jnp.dot(both, shift, preferred_element_type=f32)
        for v in range(8 // 4):
            mixed = []
            gates = []
            for k in range(4 * v, 4 * v + 4):
                limit = jnp.broadcast_to(reach_ref[pl.ds(8 * u + k, 1), :], (24, LANES))
                total = now[k].astype(f32) * taps_ref[0]
                for j in range(1, TAPS):
                    part = delayed[24 * k : 24 * k + 24, LANES * (j - 1) : LANES * j]
                    total = total + jnp.where(limit >= j, part, 0.0) * taps_ref[j]
                gates.append(total[:8])
                mixed.append(total[8:16] * total[16:])
            first = jnp.concatenate(mixed[:2], axis=1)
            second = jnp.concatenate(mixed[2:], axis=1)
            at = pl.ds(128 + 32 * u + 16 * v, 16)
            rows_ref[at, 0:256] = jnp.concatenate([first, second], axis=0).astype(bf16)
            rows_ref[at, 256:512] = jnp.concatenate([last, first], axis=0).astype(bf16)
            gate_ref[2 * u + v] = jnp.concatenate(
                [jnp.concatenate(gates[:2], axis=1), jnp.concatenate(gates[2:], axis=1)], axis=0
            ).astype(bf16)
            last = second
        return last

    placed_ref[0] = jnp.zeros((24, LANES), bf16)
    last = jnp.zeros((8, 256), f32)
    for u in range(16):
        for k in range(8):
            gather(8 * u + k)
        last = short(u, last)

    upper = col >= row
    skew = jnp.zeros((LANES, LANES), f32)
    block = jnp.zeros((LANES, LANES), bf16)
    for f in range(0, 32, 2):
        begin = 16 * f
        left, right = [], []
        for g in (f, f + 1):
            at = 128 + begin - 16 * g
            left.append(rows_ref[at : at + 512 - begin, :])
            made = [block]
            for k in range(4):
                line = jnp.broadcast_to(lags_ref[g, k : k + 1, :], (LANES, LANES))
                before, skew = skew, pltpu.roll(line, 0, 1, stride=1, stride_axis=0)
                made.append(jnp.where(upper, skew, before).astype(bf16))
            block = made[4]
            right.append(
                jnp.concatenate(
                    [
                        jnp.concatenate([made[k] for k in (1, 0, 3, 2)], axis=0),
                        jnp.concatenate([made[k] for k in (2, 1, 4, 3)], axis=0),
                    ],
                    axis=1,
                )
            )
        product = jnp.dot(
            jnp.concatenate(left, axis=1),
            jnp.concatenate(right, axis=0),
            preferred_element_type=f32,
        )
        if f == 0:
            acc_ref[...] = product
        else:
            acc_ref[begin:, :] += product

    def finish(u, carry):
        at = pl.ds(16 * u, 16)
        here = pl.ds(128 + 16 * u, 16)
        total = acc_ref[at, :] + skip * rows_ref[here, 0:256].astype(f32)
        out_ref[u] = (gate_ref[u].astype(f32) * total).astype(bf16)
        return carry

    for u in range(32):
        finish(u, 0)


def conv_rows(table, recv, filters, skips):
    whole = pl.BlockSpec(memory_space=pltpu.VMEM)
    return pl.pallas_call(
        conv_kernel,
        in_specs=[pl.BlockSpec(memory_space=pltpu.SMEM)] + [whole] * 3,
        out_specs=whole,
        out_shape=jax.ShapeDtypeStruct((32, 16, 256), bf16),
        scratch_shapes=[
            pltpu.VMEM((640, 512), bf16),
            pltpu.VMEM((512, 256), f32),
            pltpu.VMEM((32, 16, 256), bf16),
            pltpu.VMEM((256, 24, LANES), f32),
            pltpu.VMEM((LANES + 1, 24, LANES), bf16),
            pltpu.VMEM((32, 8, LANES), f32),
            pltpu.VMEM((LANES, LANES), f32),
            pltpu.VMEM((LANES, LANES), f32),
            pltpu.VMEM((32, 256), f32),
            pltpu.VMEM((TAPS, 24, LANES), f32),
        ],
        compiler_params=vmem(24),
        name="conv_rows",
    )(table, recv, filters, skips)


def power_kernel(in_ref, out_ref):
    halves = []
    for half in range(2):
        block = in_ref[:, 8 * half : 8 * half + 8, :].astype(f32).reshape(256, 256)
        halves.append(jnp.sum(block * block, axis=0, keepdims=True))
    line = jnp.concatenate(halves, axis=1)
    for i in range(16):
        out_ref[i] = line


def power_rows(rows):
    return pl.pallas_call(
        power_kernel,
        out_shape=jax.ShapeDtypeStruct((16, 1, 512), f32),
        compiler_params=vmem(4),
        name="power_rows",
    )(rows)


def scale_kernel(in_ref, power_ref, gain_ref, out_ref, turned_ref, sems):
    power = jnp.sum(power_ref[...], axis=0)
    scale = lax.rsqrt(power / 4096.0 + 1e-06)
    gain = gain_ref[...]
    sends = []
    for half in range(2):
        block = in_ref[:, 8 * half : 8 * half + 8, :].astype(f32).reshape(256, 256)
        block = jnp.transpose(block * scale[:, 256 * half : 256 * half + 256])
        turned_ref[half] = (block * gain).astype(bf16)
        send = pltpu.make_async_copy(
            turned_ref.at[half], out_ref.at[pl.ds(256 * half, 256), :], sems.at[half]
        )
        send.start()
        sends.append(send)
    for send in sends:
        send.wait()


def scale_rows(rows, power, gain):
    whole = pl.BlockSpec(memory_space=pltpu.VMEM)
    return pl.pallas_call(
        scale_kernel,
        in_specs=[whole] * 3,
        out_specs=pl.BlockSpec(memory_space=pltpu.HBM),
        out_shape=jax.ShapeDtypeStruct((512, 256), bf16),
        scratch_shapes=[pltpu.VMEM((2, 256, 256), bf16), pltpu.SemaphoreType.DMA((2,))],
        compiler_params=vmem(4),
        name="scale_rows",
    )(rows, power, gain)


def exchange(block, axis):
    return lax.all_to_all(block, axis, split_axis=0, concat_axis=0, tiled=True)


def local(
    loaded, dest_tiles, tile_counts, segments, short_filters, long_filters, skip_gain, norm_gain
):
    recv = exchange(
        pack(dest_tiles, tile_counts, loaded, long_filters, segments.reshape(4, LANES)), "seq"
    )

    placed = (recv[:, 197, :32].astype(f32) + recv[:, 198, :32].astype(f32)).astype(jnp.int32)
    placed = placed.reshape(-1)
    tiles = jnp.arange(512, dtype=jnp.int32)
    slot_ids = jnp.arange(1024, dtype=jnp.int32)
    table = jnp.sum(
        jnp.where(placed[None, :] == tiles[:, None], slot_ids[None, :], 0), axis=1
    ).astype(jnp.int32)

    gated = conv_rows(table, recv, short_filters, skip_gain.reshape(1, 256))
    mine = exchange(gated, "seq")
    every = exchange(power_rows(mine), "chan")
    return scale_rows(mine, every, norm_gain.reshape(1, 256))


def solution(mesh):
    return jax.shard_map(
        local,
        mesh=mesh,
        in_specs=(
            P(None, "seq", "chan"),
            P("seq"),
            P("seq"),
            P("seq"),
            P(None, None, "chan"),
            P("chan", "seq"),
            P("chan"),
            P("chan"),
        ),
        out_specs=P("seq", "chan"),
        check_vma=False,
    )
```
